32 devices in a mesh: groups: 2 (over y), ctx: 8 (over z, x), col: 2 (over core).
Axes of the slice: x: 2, y: 2, z: 4, core: 2. Of those that a mesh axis runs over, the one named last changes fastest.
Arguments:
- activations: bfloat16 [2048, 4096], P(('groups', 'ctx'), 'col'), parts along dimension 0, may hold values from -6 to 6
- gradients: bfloat16 [2048, 14336], P(('groups', 'ctx'), 'col'), parts along dimension 0, may hold values from -6 to 6
- doc_ids: int32 [2048], P(('groups', 'ctx')), parts along dimension 0, may hold values from 0 to 11, as said below
- proj_in: bfloat16 [4096, 64], P('col'), may hold values from -0.046875 to 0.046875
- proj_out: bfloat16 [14336, 64], P('col'), may hold values from -0.0234375 to 0.0234375
- inverse: float32 [4096, 4096], P('col', 'ctx')
- store_rows: bfloat16 [2048, 4096], P(('groups', 'ctx', 'col')), parts along dimension 0, may hold values from -0.09375 to 0.09375
Outputs:
- scores: float32 [12, 2048], P(None, ('groups', 'ctx', 'col')), parts along dimension 1
The draws below stay inside these ranges and needn't reach their ends.
There are 2 independent parts, one for each index of `groups`. The reference program is written for one: setup_inputs(seed, part) draws one part's arguments, and reference() takes and returns one part's arrays. A program takes and returns all parts, laid end to end along the dimension named above; an argument that names none is the same for every part. Nothing has to cross between parts.
Inputs may be any that keep to these rules, and one draw needn't show every extreme that they name: `doc_ids`: document numbers never fall and rise by at most one from a token to the next, starting at 0. Every aligned block of 128 tokens holds the last token of one or two documents; the last token of the sequence ends document 12 - 1.
All inputs are finite; a program needn't handle non-finite values.
Results may differ from the reference program's by a relative error of at most 0.0029.
Values may be sent and summed in bfloat16 or wider, within the bound.
No kernel may reach another device: no remote copies, remote signals or barrier semaphores. Data moves between devices by JAX's collectives and lax.ppermute only.
A program may use at most 64 MiB of HBM per device.

```python
import jax
import jax.numpy as jnp
from jax import lax

D = 4096
FF = 14336
R = 64
F = 4096
TOK_DEV = 128
TOKENS = 1024
NDOC = 12
STORE = 1024


def draw_doc_ids(key, part):
    block_count = TOKENS // TOK_DEV
    key_perm = jax.random.fold_in(key, 11)
    key_late = jax.random.fold_in(key, 12)
    key_early = jax.random.fold_in(key, 13)
    ranking = jax.random.permutation(key_perm, block_count)
    has_two = ranking < block_count // 2
    late_end = jax.random.randint(key_late, (block_count,), TOK_DEV // 2, TOK_DEV)
    late_end = jnp.where(jnp.arange(block_count) == block_count - 1, TOK_DEV - 1, late_end)
    early_end = jax.random.randint(key_early, (block_count,), 0, TOK_DEV // 2)
    position = jnp.arange(TOK_DEV)[None, :]
    is_end = (position == late_end[:, None]) | has_two[:, None] & (position == early_end[:, None])
    flat_end = is_end.reshape(TOKENS).astype(jnp.int32)
    return (jnp.cumsum(flat_end) - flat_end).astype(jnp.int32)


def draw_inverse(key, part):
    key_diag = jax.random.fold_in(key, 21)
    key_off = jax.random.fold_in(key, 22)
    diagonal = jnp.exp(jax.random.uniform(key_diag, (F,), jnp.float32, jnp.log(0.5), jnp.log(2.0)))
    offdiag = jax.random.normal(key_off, (F, F), jnp.float32) * (0.5 / jnp.sqrt(jnp.float32(F)))
    matrix = offdiag + jnp.diag(diagonal)
    return matrix.astype(jnp.float32)


def steps_of(rng, dims, cuts, low, largest):
    factor_of = 1.0
    for axis_at, blocks in cuts:
        steps = jax.random.uniform(jax.random.fold_in(jax.random.fold_in(rng, 6), axis_at), (blocks,), jnp.float32, low / len(cuts), largest / len(cuts))
        factor_of = factor_of * jnp.repeat(jnp.exp(steps), dims[axis_at] // blocks).reshape((-1,) + (1,) * (len(dims) - 1 - axis_at))
    return factor_of


def centred(key, shape, deviation, most, cuts=(), kind=jnp.bfloat16):
    level = steps_of(key, shape, cuts, -0.22, 0.18) if cuts else 1.0
    result = jax.random.normal(key, shape, jnp.float32) * deviation * level
    return jnp.minimum(jnp.maximum(result, -most), most).astype(kind)


def setup_inputs(seed: int = 0, part: int = 0) -> dict:
    keys = jax.random.split(jax.random.key(seed), 8)
    part_keys = jax.random.split(jax.random.fold_in(keys[7], part), 8)
    activations = centred(part_keys[0], (TOKENS, D), 1.0, 6.0, ((0, 8), (1, 2)))
    gradients = centred(part_keys[1], (TOKENS, FF), 1.0, 6.0, ((0, 8), (1, 2)))
    doc_ids = draw_doc_ids(jax.random.fold_in(jax.random.fold_in(keys[7], part), 71), part)
    proj_in = centred(keys[3], (D, R), (4 * D) ** -0.5, 0.046875, ((0, 2),))
    proj_out = centred(keys[4], (FF, R), (4 * FF) ** -0.5, 0.0234375, ((0, 2),))
    inverse = draw_inverse(jax.random.fold_in(keys[7], 71), part)
    store_rows = centred(part_keys[6], (STORE, F), F ** -0.5, 0.09375, ((0, 16),))
    return {"activations": activations, "gradients": gradients, "doc_ids": doc_ids, "proj_in": proj_in, "proj_out": proj_out, "inverse": inverse, "store_rows": store_rows}


def reference(activations, gradients, doc_ids, proj_in, proj_out, inverse, store_rows):
    proj_left = jnp.dot(activations, proj_in, preferred_element_type=jnp.float32)
    proj_right = jnp.dot(gradients, proj_out, preferred_element_type=jnp.float32)
    token_count = proj_left.shape[0]
    proj_rank = proj_left.shape[1]
    col_blocks = proj_left.reshape(token_count, proj_rank // 8, 8).transpose(1, 0, 2)

    def per_block(block_left):
        outer_rows = (block_left[:, :, None] * proj_right[:, None, :]).reshape(token_count, 8 * proj_rank)
        return jax.ops.segment_sum(outer_rows, doc_ids, num_segments=NDOC)

    block_sums = lax.map(per_block, col_blocks)
    doc_grads = block_sums.transpose(1, 0, 2).reshape(NDOC, proj_rank * proj_rank)
    precond = jnp.dot(doc_grads, inverse, precision=lax.Precision.HIGHEST, preferred_element_type=jnp.float32).astype(jnp.bfloat16)
    return jnp.dot(precond, store_rows.T, preferred_element_type=jnp.float32)
```

```python
import jax
import jax.numpy as jnp
from jax import lax
from jax.sharding import PartitionSpec as P


def swap(block, axis, distance):
    size = lax.axis_size(axis)
    return lax.ppermute(block, axis, [(i, i ^ distance) for i in range(size)])


def gather_blocks(block, axis):
    index = lax.axis_index(axis)
    distance = 1
    while distance < lax.axis_size(axis):
        other = swap(block, axis, distance)
        upper = (index & distance) != 0
        block = jnp.where(
            upper, jnp.concatenate([other, block]), jnp.concatenate([block, other])
        )
        distance *= 2
    return block


def shards(activations, gradients, doc_ids, proj_in, proj_out, inverse, store_rows):
    left_part = jnp.dot(activations, proj_in, preferred_element_type=jnp.float32)
    right_part = jnp.dot(gradients, proj_out, preferred_element_type=jnp.float32)
    parts = jnp.concatenate([left_part, right_part], 1)
    both = parts + swap(parts, "col", 1)
    rank = proj_in.shape[1]
    proj_left, proj_right = both[:, :rank], both[:, rank:]
    half = rank // lax.axis_size("col")
    own_half = lax.dynamic_slice_in_dim(proj_left, lax.axis_index("col") * half, half, 1)
    first_doc = doc_ids[0]
    slot = doc_ids - first_doc
    onehot = (slot[:, None] == jnp.arange(3, dtype=jnp.int32)[None, :]).astype(jnp.float32)
    weighted = (onehot[:, :, None] * own_half[:, None, :]).reshape(own_half.shape[0], 3 * half)
    local = lax.dot_general(
        weighted,
        proj_right,
        (((0,), (0,)), ((), ())),
        precision=lax.Precision.HIGHEST,
        preferred_element_type=jnp.float32,
    ).reshape(3, half * rank)
    ctx = lax.axis_size("ctx")
    numbers = jnp.full((1, half * rank), first_doc.astype(jnp.float32))
    rows = jnp.concatenate([local, numbers])[None]
    gathered = gather_blocks(rows, "ctx")
    owners = gathered[:, 3, 0]
    doc_count = 3 * ctx // 2
    docs = jnp.arange(doc_count, dtype=jnp.int32).astype(jnp.float32)
    slots = jnp.arange(3, dtype=jnp.int32).astype(jnp.float32)
    pick = (owners[None, :, None] + slots[None, None, :] == docs[:, None, None]).astype(jnp.float32)
    doc_grads = lax.dot_general(
        pick.reshape(doc_count, ctx * 3),
        gathered[:, :3].reshape(ctx * 3, half * rank),
        (((1,), (0,)), ((), ())),
        precision=lax.Precision.HIGHEST,
        preferred_element_type=jnp.float32,
    )
    partial_q = jnp.dot(
        doc_grads, inverse, precision=lax.Precision.HIGHEST, preferred_element_type=jnp.float32
    )
    precond = (partial_q + swap(partial_q, "col", 1)).astype(jnp.bfloat16)
    whole = gather_blocks(precond[None], "ctx")
    whole = whole.transpose(1, 0, 2).reshape(doc_count, -1)
    return lax.dot_general(
        whole, store_rows, (((1,), (1,)), ((), ())), preferred_element_type=jnp.float32
    )


def solution(mesh):
    in_specs = (
        P(("groups", "ctx"), "col"),
        P(("groups", "ctx"), "col"),
        P(("groups", "ctx")),
        P("col", None),
        P("col", None),
        P("col", "ctx"),
        P(("groups", "ctx", "col"), None),
    )
    out_specs = P(None, ("groups", "ctx", "col"))
    return jax.shard_map(shards, mesh=mesh, in_specs=in_specs, out_specs=out_specs, check_vma=False)
```

```python
import functools

import jax
import jax.numpy as jnp
from jax import lax
from jax.experimental import pallas as pl
from jax.experimental.pallas import tpu as pltpu
from jax.sharding import PartitionSpec as P

SLOTS = 3
LANES = 128


def distances(axis):
    size = lax.axis_size(axis)
    return [size >> step for step in range(1, size.bit_length())]


def swap(block, distance, cross):
    ctx, col = lax.axis_size("ctx"), lax.axis_size("col")
    route = [
        (c * col + p, (c ^ distance) * col + (p ^ cross)) for c in range(ctx) for p in range(col)
    ]
    return lax.ppermute(block, ("ctx", "col"), route)


def ordered(own, other, distance):
    upper = (lax.axis_index("ctx") & distance) != 0
    return jnp.where(upper, jnp.concatenate([other, own]), jnp.concatenate([own, other]))


def position():
    index, place = lax.axis_index("ctx"), 0
    for step, distance in enumerate(distances("ctx")):
        place = place + jnp.where((index & distance) != 0, 1 << step, 0)
    return place


def project_kernel(chunks, ids_hbm, act_hbm, pin_hbm, grad_hbm, pout_hbm, out, mask, ids, act, pin, grad, pout, sems):
    depth = grad.shape[1] // chunks
    copies = [
        pltpu.make_async_copy(act_hbm, act, sems.at[0]),
        pltpu.make_async_copy(pin_hbm, pin, sems.at[1]),
    ]
    for n in range(chunks):
        part = pl.ds(n * depth, depth)
        copies.append(pltpu.make_async_copy(pout_hbm.at[:, part], pout.at[:, part], sems.at[2 + 2 * n]))
        copies.append(pltpu.make_async_copy(grad_hbm.at[:, part], grad.at[:, part], sems.at[3 + 2 * n]))
    copies.append(pltpu.make_async_copy(ids_hbm, ids, sems.at[2 + 2 * chunks]))
    for copy in copies:
        copy.start()
    rank = pin.shape[0]
    dims = (((1,), (1,)), ((), ()))
    copies[0].wait()
    copies[1].wait()
    out[:rank, :] = lax.dot_general(pin[...], act[...], dims, preferred_element_type=jnp.float32)
    total = None
    for n in range(chunks):
        copies[2 + 2 * n].wait()
        copies[3 + 2 * n].wait()
        part = pl.ds(n * depth, depth)
        term = lax.dot_general(pout[:, part], grad[:, part], dims, preferred_element_type=jnp.float32)
        total = term if total is None else total + term
    out[rank:, :] = total
    copies[-1].wait()
    first = ids[:, :1]
    rows = lax.broadcasted_iota(jnp.int32, mask.shape, 0)
    tokens = jnp.broadcast_to(ids[...], mask.shape)
    heads = jnp.broadcast_to(first, mask.shape)
    hit = (tokens - heads == rows).astype(jnp.float32)
    mask[...] = jnp.where(rows == mask.shape[0] - 1, heads.astype(jnp.float32), hit)


def project(activations, gradients, proj_in, proj_out, doc_ids):
    tokens, depth = gradients.shape
    rank = proj_in.shape[1]
    chunks = max(n for n in (4, 2, 1) if depth % (n * LANES) == 0)
    anywhere = pl.BlockSpec(memory_space=pl.ANY)
    vmem = pl.BlockSpec(memory_space=pltpu.VMEM)
    return pl.pallas_call(
        functools.partial(project_kernel, chunks),
        out_shape=(
            jax.ShapeDtypeStruct((2 * rank, tokens), jnp.float32),
            jax.ShapeDtypeStruct((8, tokens), jnp.float32),
        ),
        in_specs=[anywhere] * 5,
        out_specs=(vmem, vmem),
        scratch_shapes=[
            pltpu.VMEM((1, tokens), jnp.int32),
            pltpu.VMEM(activations.shape, jnp.bfloat16),
            pltpu.VMEM(proj_in.shape[::-1], jnp.bfloat16),
            pltpu.VMEM(gradients.shape, jnp.bfloat16),
            pltpu.VMEM(proj_out.shape[::-1], jnp.bfloat16),
            pltpu.SemaphoreType.DMA((3 + 2 * chunks,)),
        ],
    )(doc_ids.reshape(1, tokens), activations, proj_in.T, gradients, proj_out.T)


def split(array):
    high = lax.reduce_precision(array, 8, 7)
    return high.astype(jnp.bfloat16), (array - high).astype(jnp.bfloat16)


def shards(activations, gradients, doc_ids, proj_in, proj_out, inverse, store_rows):
    ctx = lax.axis_size("ctx")
    rank = proj_in.shape[1]
    half = rank // lax.axis_size("col")
    doc_count = SLOTS * ctx // 2
    inverse_high, inverse_low = split(inverse)

    part, mask = project(activations, gradients, proj_in, proj_out, doc_ids)
    both = part + swap(part, 0, 1)
    own_half = lax.dynamic_slice_in_dim(both, lax.axis_index("col") * half, half, 0)
    weighted = (mask[:SLOTS, None, :] * own_half[None]).reshape(SLOTS * half, -1)
    local = lax.dot_general(
        weighted,
        both[rank:],
        (((1,), (1,)), ((), ())),
        precision=lax.Precision.HIGHEST,
        preferred_element_type=jnp.float32,
    )
    blocks = local.reshape(-1, LANES)
    places = 8 * LANES
    place = jnp.arange(places, dtype=jnp.int32) - SLOTS * position()
    first = mask[-1, 0]
    numbers = jnp.where((place >= 0) & (place < SLOTS), first + place.astype(jnp.float32), 0.0)
    numbers = numbers.reshape(8, LANES)
    for distance in distances("ctx"):
        size = blocks.shape[0]
        other = swap(jnp.concatenate([blocks, numbers]), distance, 0)
        blocks = ordered(blocks, other[:size], distance)
        numbers = numbers + other[size:]
    if SLOTS * ctx <= LANES:
        numbers = numbers[0]
    numbers = numbers.reshape(-1)[: SLOTS * ctx]
    docs = jnp.arange(doc_count, dtype=jnp.int32).astype(jnp.float32)
    pick = (numbers[None, :] == docs[:, None]).astype(jnp.float32)
    pieces = blocks.reshape(SLOTS * ctx, half * rank)
    pieces_high, pieces_low = split(pieces)
    terms = jnp.dot(
        jnp.concatenate([pieces_high, pieces_low]), inverse_high, preferred_element_type=jnp.float32
    )
    small = jnp.dot(pieces_high, inverse_low, preferred_element_type=jnp.float32)
    terms = terms[: SLOTS * ctx] + (terms[SLOTS * ctx :] + small)
    partial_q = jnp.dot(
        pick, terms, precision=lax.Precision.HIGHEST, preferred_element_type=jnp.float32
    )
    precond = (partial_q + swap(partial_q, 0, 1)).astype(jnp.bfloat16)
    width = precond.shape[1]
    whole = precond.reshape(-1, min(width, LANES))
    for distance in distances("ctx"):
        whole = ordered(whole, swap(whole, distance, 1), distance)
    bits = len(distances("ctx"))
    whole = whole.reshape((2,) * bits + (doc_count, width))
    whole = whole.transpose((bits,) + tuple(range(bits))[::-1] + (bits + 1,)).reshape(doc_count, -1)
    return lax.dot_general(
        whole, store_rows, (((1,), (1,)), ((), ())), preferred_element_type=jnp.float32
    )


def solution(mesh):
    in_specs = (
        P(("groups", "ctx"), "col"),
        P(("groups", "ctx"), "col"),
        P(("groups", "ctx")),
        P("col", None),
        P("col", None),
        P("col", "ctx"),
        P(("groups", "ctx", "col"), None),
    )
    out_specs = P(None, ("groups", "ctx", "col"))
    return jax.shard_map(shards, mesh=mesh, in_specs=in_specs, out_specs=out_specs, check_vma=False)
```

```python
import functools

import jax
import jax.numpy as jnp
from jax import lax
from jax.experimental import pallas as pl
from jax.experimental.pallas import tpu as pltpu
from jax.sharding import PartitionSpec as P

SLOTS = 3
LANES = 128
VMEM_LIMIT = 16 << 20


def distances(axis):
    size = lax.axis_size(axis)
    return [size >> step for step in range(1, size.bit_length())]


def swap(block, distance, cross):
    ctx, col = lax.axis_size("ctx"), lax.axis_size("col")
    route = [
        (c * col + p, (c ^ distance) * col + (p ^ cross)) for c in range(ctx) for p in range(col)
    ]
    return lax.ppermute(block, ("ctx", "col"), route)


def ordered(own, other, distance):
    upper = (lax.axis_index("ctx") & distance) != 0
    return jnp.where(upper, jnp.concatenate([other, own]), jnp.concatenate([own, other]))


def position():
    index, place = lax.axis_index("ctx"), 0
    for step, distance in enumerate(distances("ctx")[:-1]):
        place = place + jnp.where((index & distance) != 0, 1 << step, 0)
    return place


def kept(space, *arrays):
    return [pltpu.with_memory_space_constraint(array, space) for array in arrays]


def fetch_kernel(pieces, array, after, out, sems):
    rows = out.shape[0] // pieces
    copies = [
        pltpu.make_async_copy(array.at[pl.ds(n * rows, rows), :], out.at[pl.ds(n * rows, rows), :], sems.at[n])
        for n in range(pieces)
    ]
    for copy in copies:
        copy.start()
    for copy in copies:
        copy.wait()


def fetch(array, after):
    pieces = 4
    return pl.pallas_call(
        functools.partial(fetch_kernel, pieces),
        out_shape=pltpu.VMEM(array.shape, array.dtype),
        in_specs=[pl.BlockSpec(memory_space=pltpu.HBM), pl.BlockSpec(memory_space=pltpu.VMEM)],
        out_specs=pl.BlockSpec(memory_space=pltpu.VMEM),
        scratch_shapes=[pltpu.SemaphoreType.DMA((pieces,))],
        compiler_params=pltpu.CompilerParams(vmem_limit_bytes=VMEM_LIMIT),
    )(*kept(pltpu.HBM, array), *kept(pltpu.VMEM, after))


def project_kernel(chunks, ids_hbm, act_hbm, pin_hbm, grad_hbm, pout_hbm, out, mask, numbers, ids, act, pin, grad, pout, sems):
    depth = grad.shape[1] // chunks
    copies = [
        pltpu.make_async_copy(act_hbm, act, sems.at[0]),
        pltpu.make_async_copy(pin_hbm, pin, sems.at[1]),
    ]
    for n in range(chunks):
        part = pl.ds(n * depth, depth)
        copies.append(pltpu.make_async_copy(pout_hbm.at[:, part], pout.at[:, part], sems.at[2 + 2 * n]))
        copies.append(pltpu.make_async_copy(grad_hbm.at[:, part], grad.at[:, part], sems.at[3 + 2 * n]))
    copies.append(pltpu.make_async_copy(ids_hbm, ids, sems.at[2 + 2 * chunks]))
    for copy in copies:
        copy.start()
    rank = pin.shape[0]
    dims = (((1,), (1,)), ((), ()))
    copies[0].wait()
    copies[1].wait()
    out[:rank, :] = lax.dot_general(pin[...], act[...], dims, preferred_element_type=jnp.float32)
    total = None
    for n in range(chunks):
        copies[2 + 2 * n].wait()
        copies[3 + 2 * n].wait()
        part = pl.ds(n * depth, depth)
        term = lax.dot_general(pout[:, part], grad[:, part], dims, preferred_element_type=jnp.float32)
        total = term if total is None else total + term
    out[rank:, :] = total
    copies[-1].wait()
    rows = lax.broadcasted_iota(jnp.int32, mask.shape, 0)
    first = jnp.broadcast_to(ids[:, :1], mask.shape)
    mask[...] = (jnp.broadcast_to(ids[...], mask.shape) - first == rows).astype(jnp.float32)
    shape = numbers.shape
    place = lax.broadcasted_iota(jnp.int32, shape, 0) * LANES + lax.broadcasted_iota(jnp.int32, shape, 1)
    place = place - SLOTS * position()
    owned = (place >= 0) & (place < SLOTS)
    first = jnp.broadcast_to(ids[:, :1], shape)
    numbers[...] = jnp.where(owned, first + place, 0).astype(jnp.float32)


def project(activations, gradients, proj_in, proj_out, doc_ids):
    tokens, depth = gradients.shape
    rank = proj_in.shape[1]
    chunks = max(n for n in (4, 2, 1) if depth % (n * LANES) == 0)
    hbm = pl.BlockSpec(memory_space=pltpu.HBM)
    vmem = pl.BlockSpec(memory_space=pltpu.VMEM)
    return pl.pallas_call(
        functools.partial(project_kernel, chunks),
        out_shape=(
            pltpu.VMEM((2 * rank, tokens), jnp.float32),
            pltpu.VMEM((8, tokens), jnp.float32),
            pltpu.VMEM((8, LANES), jnp.float32),
        ),
        in_specs=[hbm] * 5,
        out_specs=(vmem, vmem, vmem),
        scratch_shapes=[
            pltpu.VMEM((1, tokens), jnp.int32),
            pltpu.VMEM(activations.shape, jnp.bfloat16),
            pltpu.VMEM(proj_in.shape[::-1], jnp.bfloat16),
            pltpu.VMEM(gradients.shape, jnp.bfloat16),
            pltpu.VMEM(proj_out.shape[::-1], jnp.bfloat16),
            pltpu.SemaphoreType.DMA((3 + 2 * chunks,)),
        ],
        compiler_params=pltpu.CompilerParams(vmem_limit_bytes=VMEM_LIMIT),
    )(*kept(pltpu.HBM, doc_ids.reshape(1, tokens), activations, proj_in.T, gradients, proj_out.T))


def split(array):
    high = array.astype(jnp.bfloat16)
    return high, (array - high.astype(jnp.float32)).astype(jnp.bfloat16)


def precondition_kernel(own, other, inverse, out, pieces):
    depth = inverse.shape[0]
    size = own.shape[0] - 8
    count = size * LANES // depth
    room = pieces.shape[0] // 2
    pieces[...] = jnp.zeros_like(pieces)
    for k in range(depth // LANES):
        for n, part in enumerate((own, other)):
            pieces[pl.ds(n * room, count), pl.ds(k * LANES, LANES)] = part[
                pl.ds(k, count, stride=depth // LANES), :
            ]
    step = 2 * LANES if depth % (2 * LANES) == 0 else LANES
    total = None
    for n in range(depth // step):
        at = pl.ds(n * step, step)
        high, low = split(pieces[:, at])
        weights_high, weights_low = split(inverse[at, :])
        first = jnp.dot(
            jnp.concatenate([high, low]), weights_high, preferred_element_type=jnp.float32
        )
        second = jnp.dot(high, weights_low, preferred_element_type=jnp.float32)
        term = first[: 2 * room] + (first[2 * room :] + second)
        total = term if total is None else total + term
    docs = lax.broadcasted_iota(jnp.int32, (out.shape[0], count), 0).astype(jnp.float32)
    result = None
    for n, part in enumerate((own, other)):
        lanes = jnp.concatenate(
            [part[size + r : size + r + 1, :] for r in range(pl.cdiv(count, LANES))], 1
        )[:, :count]
        pick = (jnp.broadcast_to(lanes, docs.shape) == docs).astype(jnp.float32)
        term = jnp.dot(
            pick,
            total[n * room : n * room + count],
            precision=lax.Precision.HIGHEST,
            preferred_element_type=jnp.float32,
        )
        result = term if result is None else result + term
    out[...] = result


def precondition(own, other, inverse, doc_count):
    vmem = pl.BlockSpec(memory_space=pltpu.VMEM)
    count = (own.shape[0] - 8) * LANES // inverse.shape[0]
    return pl.pallas_call(
        precondition_kernel,
        out_shape=pltpu.VMEM((doc_count, inverse.shape[1]), jnp.float32),
        in_specs=[vmem] * 3,
        out_specs=vmem,
        scratch_shapes=[pltpu.VMEM((2 * pl.cdiv(count, 8) * 8, inverse.shape[0]), jnp.float32)],
        compiler_params=pltpu.CompilerParams(vmem_limit_bytes=VMEM_LIMIT),
    )(*kept(pltpu.VMEM, own, other, inverse))


def shards(activations, gradients, doc_ids, proj_in, proj_out, inverse, store_rows):
    ctx = lax.axis_size("ctx")
    rank = proj_in.shape[1]
    half = rank // lax.axis_size("col")
    doc_count = SLOTS * ctx // 2
    part, mask, numbers = project(activations, gradients, proj_in, proj_out, doc_ids)
    both = part + swap(part, 0, 1)
    own_half = lax.dynamic_slice_in_dim(both, lax.axis_index("col") * half, half, 0)
    weighted = (mask[:SLOTS, None, :] * own_half[None]).reshape(SLOTS * half, -1)
    local = lax.dot_general(
        weighted,
        both[rank:],
        (((1,), (1,)), ((), ())),
        precision=lax.Precision.HIGHEST,
        preferred_element_type=jnp.float32,
    )
    blocks = local.reshape(-1, LANES)
    payload = jnp.concatenate([blocks, numbers])
    for distance in distances("ctx")[:-1]:
        size = payload.shape[0] - 8
        other = swap(payload, distance, 0)
        blocks = ordered(payload[:size], other[:size], distance)
        payload = jnp.concatenate([blocks, payload[size:] + other[size:]])
    other = swap(payload, distances("ctx")[-1], 0)
    inside = fetch(inverse, payload)
    other, inside = lax.optimization_barrier((other, inside))
    partial_q = precondition(payload, other, inside, doc_count)
    precond = (partial_q + swap(partial_q, 0, 1)).astype(jnp.bfloat16)
    width = precond.shape[1]
    whole = precond.reshape(-1, min(width, LANES))
    for distance in distances("ctx"):
        whole = ordered(whole, swap(whole, distance, 1), distance)
    bits = len(distances("ctx"))
    whole = whole.reshape((2,) * bits + (doc_count, width))
    whole = whole.transpose((bits,) + tuple(range(bits))[::-1] + (bits + 1,)).reshape(doc_count, -1)
    return lax.dot_general(
        whole, store_rows, (((1,), (1,)), ((), ())), preferred_element_type=jnp.float32
    )


def solution(mesh):
    in_specs = (
        P(("groups", "ctx"), "col"),
        P(("groups", "ctx"), "col"),
        P(("groups", "ctx")),
        P("col", None),
        P("col", None),
        P("col", "ctx"),
        P(("groups", "ctx", "col"), None),
    )
    out_specs = P(None, ("groups", "ctx", "col"))
    return jax.shard_map(shards, mesh=mesh, in_specs=in_specs, out_specs=out_specs, check_vma=False)
```

```python
import functools

import jax
import jax.numpy as jnp
from jax import lax
from jax.experimental import pallas as pl
from jax.experimental.pallas import tpu as pltpu
from jax.sharding import PartitionSpec as P

SLOTS = 3
LANES = 128
TOP = 13.0
VMEM_LIMIT = 16 << 20


def distances(axis):
    size = lax.axis_size(axis)
    return [size >> step for step in range(1, size.bit_length())]


def swap(block, distance, cross):
    ctx, col = lax.axis_size("ctx"), lax.axis_size("col")
    route = [
        (c * col + p, (c ^ distance) * col + (p ^ cross)) for c in range(ctx) for p in range(col)
    ]
    return lax.ppermute(block, ("ctx", "col"), route)


def ordered(own, other, distance):
    upper = (lax.axis_index("ctx") & distance) != 0
    return jnp.where(upper, jnp.concatenate([other, own]), jnp.concatenate([own, other]))


def position():
    index, place = lax.axis_index("ctx"), 0
    for step, distance in enumerate(distances("ctx")[:-1]):
        place = place + jnp.where((index & distance) != 0, 1 << step, 0)
    return place


def kept(space, *arrays):
    return [pltpu.with_memory_space_constraint(array, space) for array in arrays]


def fetch_kernel(start, pieces, array, after, out, sems):
    rows = out.shape[0] // pieces
    copies = [
        pltpu.make_async_copy(
            array.at[pl.ds(start + n * rows, rows), :], out.at[pl.ds(n * rows, rows), :], sems.at[n]
        )
        for n in range(pieces)
    ]
    for copy in copies:
        copy.start()
    for copy in copies:
        copy.wait()


def fetch(array, start, rows, after):
    pieces = 2
    return pl.pallas_call(
        functools.partial(fetch_kernel, start, pieces),
        out_shape=pltpu.VMEM((rows, array.shape[1]), array.dtype),
        in_specs=[pl.BlockSpec(memory_space=pltpu.HBM), pl.BlockSpec(memory_space=pltpu.VMEM)],
        out_specs=pl.BlockSpec(memory_space=pltpu.VMEM),
        scratch_shapes=[pltpu.SemaphoreType.DMA((pieces,))],
        compiler_params=pltpu.CompilerParams(vmem_limit_bytes=VMEM_LIMIT),
    )(*kept(pltpu.HBM, array), *kept(pltpu.VMEM, after))


def project_kernel(chunks, ids_hbm, act_hbm, pin_hbm, grad_hbm, pout_hbm, out, mask, numbers, ids, act, pin, grad, pout, sems):
    depth = grad.shape[1] // chunks
    copies = [
        pltpu.make_async_copy(act_hbm, act, sems.at[0]),
        pltpu.make_async_copy(pin_hbm, pin, sems.at[1]),
    ]
    for n in range(chunks):
        part = pl.ds(n * depth, depth)
        copies.append(pltpu.make_async_copy(pout_hbm.at[:, part], pout.at[:, part], sems.at[2 + 2 * n]))
        copies.append(pltpu.make_async_copy(grad_hbm.at[:, part], grad.at[:, part], sems.at[3 + 2 * n]))
    copies.append(pltpu.make_async_copy(ids_hbm, ids, sems.at[2 + 2 * chunks]))
    for copy in copies:
        copy.start()
    rank = pin.shape[0]
    dims = (((1,), (1,)), ((), ()))
    copies[0].wait()
    copies[1].wait()
    out[:rank, :] = lax.dot_general(pin[...], act[...], dims, preferred_element_type=jnp.float32)
    total = None
    for n in range(chunks):
        copies[2 + 2 * n].wait()
        copies[3 + 2 * n].wait()
        part = pl.ds(n * depth, depth)
        term = lax.dot_general(pout[:, part], grad[:, part], dims, preferred_element_type=jnp.float32)
        total = term if total is None else total + term
    out[rank:, :] = total
    copies[-1].wait()
    rows = lax.broadcasted_iota(jnp.int32, mask.shape, 0)
    first = jnp.broadcast_to(ids[:, :1], mask.shape)
    mask[...] = (jnp.broadcast_to(ids[...], mask.shape) - first == rows).astype(jnp.float32)
    shape = numbers.shape
    row = lax.broadcasted_iota(jnp.int32, shape, 0)
    place = row % 4 * LANES + lax.broadcasted_iota(jnp.int32, shape, 1) - SLOTS * position()
    first = jnp.broadcast_to(ids[:, :1], shape)
    value = jnp.where(row < 4, first + place, 1)
    numbers[...] = jnp.where((place >= 0) & (place < SLOTS), value, 0).astype(jnp.float32)


def project(activations, gradients, proj_in, proj_out, doc_ids):
    tokens, depth = gradients.shape
    rank = proj_in.shape[1]
    chunks = max(n for n in (4, 2, 1) if depth % (n * LANES) == 0)
    hbm = pl.BlockSpec(memory_space=pltpu.HBM)
    vmem = pl.BlockSpec(memory_space=pltpu.VMEM)
    return pl.pallas_call(
        functools.partial(project_kernel, chunks),
        out_shape=(
            pltpu.VMEM((2 * rank, tokens), jnp.float32),
            pltpu.VMEM((8, tokens), jnp.float32),
            pltpu.VMEM((8, LANES), jnp.float32),
        ),
        in_specs=[hbm] * 5,
        out_specs=(vmem, vmem, vmem),
        scratch_shapes=[
            pltpu.VMEM((1, tokens), jnp.int32),
            pltpu.VMEM(activations.shape, jnp.bfloat16),
            pltpu.VMEM(proj_in.shape[::-1], jnp.bfloat16),
            pltpu.VMEM(gradients.shape, jnp.bfloat16),
            pltpu.VMEM(proj_out.shape[::-1], jnp.bfloat16),
            pltpu.SemaphoreType.DMA((3 + 2 * chunks,)),
        ],
        compiler_params=pltpu.CompilerParams(vmem_limit_bytes=VMEM_LIMIT),
    )(*kept(pltpu.HBM, doc_ids.reshape(1, tokens), activations, proj_in.T, gradients, proj_out.T))


def outer_kernel(part, other, mask, numbers, sums, tags, left):
    rank, tokens = left.shape
    left[...] = part[:rank, :] + other[:rank, :]
    right = part[rank:, :] + other[rank:, :]
    columns = [left[pl.ds(k, rank // 2, stride=2), :] for k in range(2)]
    weighted = jnp.concatenate(
        [jnp.concatenate([half * mask[s : s + 1, :] for half in columns], 1) for s in range(SLOTS)]
    )
    none = jnp.zeros_like(right)
    paired = jnp.concatenate(
        [jnp.concatenate([right, none], 1), jnp.concatenate([none, right], 1)]
    )
    found = lax.dot_general(
        weighted,
        paired,
        (((1,), (1,)), ((), ())),
        precision=lax.Precision.HIGHEST,
        preferred_element_type=jnp.float32,
    )
    largest = jnp.max(jnp.max(jnp.abs(found), 0, keepdims=True), 1, keepdims=True)
    power = jnp.floor(jnp.log2(jnp.maximum(largest, 1e-30)))
    sums[...] = found * jnp.exp2(TOP - power)
    rows = lax.broadcasted_iota(jnp.int32, numbers.shape, 0)
    tags[...] = numbers[...] * jnp.where(rows < 4, 1.0, jnp.broadcast_to(power, rows.shape))


def outer(part, other, mask, numbers):
    rank, tokens = part.shape[0] // 2, part.shape[1]
    vmem = pl.BlockSpec(memory_space=pltpu.VMEM)
    return pl.pallas_call(
        outer_kernel,
        out_shape=(
            pltpu.VMEM((SLOTS * rank // 2, 2 * rank), jnp.float32),
            pltpu.VMEM(numbers.shape, jnp.float32),
        ),
        in_specs=[vmem] * 4,
        out_specs=(vmem, vmem),
        scratch_shapes=[pltpu.VMEM((rank, tokens), jnp.float32)],
        compiler_params=pltpu.CompilerParams(vmem_limit_bytes=VMEM_LIMIT),
    )(*kept(pltpu.VMEM, part, other, mask, numbers))


def split(array):
    high = array.astype(jnp.bfloat16)
    return high, (array - high.astype(jnp.float32)).astype(jnp.bfloat16)


def precondition_kernel(own, other, upper, lower, out, pieces):
    depth = 2 * upper.shape[0]
    size = own.shape[0] - 8
    count = size * LANES // depth
    room = pieces.shape[0] // 2
    pieces[...] = jnp.zeros_like(pieces)
    for k in range(depth // LANES):
        for n, part in enumerate((own, other)):
            pieces[pl.ds(n * room, count), pl.ds(k * LANES, LANES)] = part[
                pl.ds(k, count, stride=depth // LANES), :
            ]
    step = 2 * LANES if depth % (4 * LANES) == 0 else LANES
    total = None
    for n in range(depth // step):
        high, low = split(pieces[:, pl.ds(n * step, step)])
        half, row = divmod(n * step, depth // 2)
        weights_high, weights_low = split((upper, lower)[half][pl.ds(row, step), :])
        first = jnp.dot(
            jnp.concatenate([high, low]), weights_high, preferred_element_type=jnp.float32
        )
        second = jnp.dot(high, weights_low, preferred_element_type=jnp.float32)
        term = first[: 2 * room] + (first[2 * room :] + second)
        total = term if total is None else total + term
    docs = lax.broadcasted_iota(jnp.int32, (out.shape[0], count), 0).astype(jnp.float32)
    result = None
    for n, part in enumerate((own, other)):
        rows = [
            [part[size + r : size + r + 1, :] for r in range(at, at + pl.cdiv(count, LANES))]
            for at in (0, 4)
        ]
        lanes, powers = (
            jnp.broadcast_to(jnp.concatenate(row, 1)[:, :count], docs.shape) for row in rows
        )
        pick = jnp.where(lanes == docs, jnp.exp2(powers - TOP), 0.0)
        term = jnp.dot(
            pick,
            total[n * room : n * room + count],
            precision=lax.Precision.HIGHEST,
            preferred_element_type=jnp.float32,
        )
        result = term if result is None else result + term
    out[...] = result


def precondition(own, other, upper, lower, doc_count):
    vmem = pl.BlockSpec(memory_space=pltpu.VMEM)
    depth, width = 2 * upper.shape[0], upper.shape[1]
    count = (own.shape[0] - 8) * LANES // depth
    return pl.pallas_call(
        precondition_kernel,
        out_shape=pltpu.VMEM((doc_count, width), jnp.float32),
        in_specs=[vmem] * 4,
        out_specs=vmem,
        scratch_shapes=[pltpu.VMEM((2 * pl.cdiv(count, 8) * 8, depth), jnp.float32)],
        compiler_params=pltpu.CompilerParams(vmem_limit_bytes=VMEM_LIMIT),
    )(*kept(pltpu.VMEM, own, other, upper, lower))


def shards(activations, gradients, doc_ids, proj_in, proj_out, inverse, store_rows):
    ctx = lax.axis_size("ctx")
    rank = proj_in.shape[1]
    half = rank // lax.axis_size("col")
    doc_count = SLOTS * ctx // 2
    part, mask, numbers = project(activations, gradients, proj_in, proj_out, doc_ids)
    sums, tags = outer(part, swap(part, 0, 1), mask, numbers)
    blocks, numbers = sums.astype(jnp.float16), tags.astype(jnp.float16)
    rows = inverse.shape[0] // 2
    for distance in distances("ctx")[:-1]:
        size = blocks.shape[0]
        payload = jnp.concatenate([blocks, numbers])
        other = swap(payload, distance, 1)
        if distance == distances("ctx")[-2]:
            upper = fetch(inverse, 0, rows, numbers.astype(jnp.float32))
            other, upper = lax.optimization_barrier((other, upper))
        blocks = ordered(blocks, other[:size], distance)
        numbers = numbers + other[size:]
    halves = blocks.reshape(-1, 2, half * rank // LANES, LANES)
    first = lax.axis_index("col") == 0
    own = jnp.where(first, halves[:, 0], halves[:, 1]).reshape(-1, LANES)
    others = jnp.where(first, halves[:, 1], halves[:, 0]).reshape(-1, LANES)
    payload = jnp.concatenate([own, numbers]).astype(jnp.float32)
    other = swap(jnp.concatenate([others, numbers]), distances("ctx")[-1], 1)
    lower = fetch(inverse, rows, rows, payload)
    other, lower = lax.optimization_barrier((other, lower))
    partial_q = precondition(payload, other.astype(jnp.float32), upper, lower, doc_count)
    precond = (partial_q + swap(partial_q, 0, 1)).astype(jnp.bfloat16)
    width = precond.shape[1]
    whole = precond.reshape(-1, min(width, LANES))
    for distance in distances("ctx"):
        whole = ordered(whole, swap(whole, distance, 1), distance)
    bits = len(distances("ctx"))
    whole = whole.reshape((2,) * bits + (doc_count, width))
    whole = whole.transpose((bits,) + tuple(range(bits))[::-1] + (bits + 1,)).reshape(doc_count, -1)
    return lax.dot_general(
        whole, store_rows, (((1,), (1,)), ((), ())), preferred_element_type=jnp.float32
    )


def solution(mesh):
    in_specs = (
        P(("groups", "ctx"), "col"),
        P(("groups", "ctx"), "col"),
        P(("groups", "ctx")),
        P("col", None),
        P("col", None),
        P("col", "ctx"),
        P(("groups", "ctx", "col"), None),
    )
    out_specs = P(None, ("groups", "ctx", "col"))
    return jax.shard_map(shards, mesh=mesh, in_specs=in_specs, out_specs=out_specs, check_vma=False)
```

```python
import functools

import jax
import jax.numpy as jnp
from jax import lax
from jax.experimental import pallas as pl
from jax.experimental.pallas import tpu as pltpu
from jax.sharding import PartitionSpec as P

SLOTS = 3
LANES = 128
TOP = 13.0
VMEM_LIMIT = 16 << 20


def far_distances():
    size = lax.axis_size("ctx")
    return [size >> step for step in range(1, size.bit_length() - 2)]


def near_distance(c, p, last):
    even = (c ^ (c >> 1) ^ p ^ last) & 1
    return 1 + even


def swap(block, partner):
    ctx, col = lax.axis_size("ctx"), lax.axis_size("col")
    route = []
    for c in range(ctx):
        for p in range(col):
            there, core = partner(c, p)
            route.append((c * col + p, there * col + core))
    return lax.ppermute(block, ("ctx", "col"), route)


def swap_cores(block):
    return swap(block, lambda c, p: (c, p ^ 1))


def swap_far(block, distance):
    return swap(block, lambda c, p: (c ^ distance, p ^ 1))


def swap_near(block, last):
    return swap(block, lambda c, p: (c ^ near_distance(c, p, last), p ^ 1))


def ordered(own, other, distance):
    upper = (lax.axis_index("ctx") & distance) != 0
    return jnp.where(upper, jnp.concatenate([other, own]), jnp.concatenate([own, other]))


def position():
    index, place = lax.axis_index("ctx"), 0
    for step, distance in enumerate(far_distances()):
        place = place + jnp.where((index & distance) != 0, 1 << step, 0)
    return place


def kept(space, *arrays):
    return [pltpu.with_memory_space_constraint(array, space) for array in arrays]


def fetch_kernel(start, pieces, array, after, out, sems):
    rows = out.shape[0] // pieces
    copies = [
        pltpu.make_async_copy(
            array.at[pl.ds(start + n * rows, rows), :], out.at[pl.ds(n * rows, rows), :], sems.at[n]
        )
        for n in range(pieces)
    ]
    for copy in copies:
        copy.start()
    for copy in copies:
        copy.wait()


def fetch(array, start, rows, after):
    pieces = 2
    return pl.pallas_call(
        functools.partial(fetch_kernel, start, pieces),
        out_shape=pltpu.VMEM((rows, array.shape[1]), array.dtype),
        in_specs=[pl.BlockSpec(memory_space=pltpu.HBM), pl.BlockSpec(memory_space=pltpu.VMEM)],
        out_specs=pl.BlockSpec(memory_space=pltpu.VMEM),
        scratch_shapes=[pltpu.SemaphoreType.DMA((pieces,))],
        compiler_params=pltpu.CompilerParams(vmem_limit_bytes=VMEM_LIMIT),
    )(*kept(pltpu.HBM, array), *kept(pltpu.VMEM, after))


def project_kernel(chunks, ids_hbm, act_hbm, pin_hbm, grad_hbm, pout_hbm, out, mask, numbers, ids, act, pin, grad, pout, sems):
    depth = grad.shape[1] // chunks
    copies = [
        pltpu.make_async_copy(act_hbm, act, sems.at[0]),
        pltpu.make_async_copy(pin_hbm, pin, sems.at[1]),
    ]
    for n in range(chunks):
        part = pl.ds(n * depth, depth)
        copies.append(pltpu.make_async_copy(pout_hbm.at[:, part], pout.at[:, part], sems.at[2 + 2 * n]))
        copies.append(pltpu.make_async_copy(grad_hbm.at[:, part], grad.at[:, part], sems.at[3 + 2 * n]))
    copies.append(pltpu.make_async_copy(ids_hbm, ids, sems.at[2 + 2 * chunks]))
    for copy in copies:
        copy.start()
    rank = pin.shape[0]
    dims = (((1,), (1,)), ((), ()))
    copies[0].wait()
    copies[1].wait()
    out[:rank, :] = lax.dot_general(pin[...], act[...], dims, preferred_element_type=jnp.float32)
    total = None
    for n in range(chunks):
        copies[2 + 2 * n].wait()
        copies[3 + 2 * n].wait()
        part = pl.ds(n * depth, depth)
        term = lax.dot_general(pout[:, part], grad[:, part], dims, preferred_element_type=jnp.float32)
        total = term if total is None else total + term
    out[rank:, :] = total
    copies[-1].wait()
    rows = lax.broadcasted_iota(jnp.int32, mask.shape, 0)
    first = jnp.broadcast_to(ids[:, :1], mask.shape)
    mask[...] = (jnp.broadcast_to(ids[...], mask.shape) - first == rows).astype(jnp.float32)
    shape = numbers.shape
    row = lax.broadcasted_iota(jnp.int32, shape, 0)
    place = row % 2 * LANES + lax.broadcasted_iota(jnp.int32, shape, 1) - SLOTS * position()
    first = jnp.broadcast_to(ids[:, :1], shape)
    value = jnp.where(row < 4, first + place, 1)
    owned = (place >= 0) & (place < SLOTS) & (row % 4 < 2)
    numbers[...] = jnp.where(owned, value, 0).astype(jnp.float32)


def project(activations, gradients, proj_in, proj_out, doc_ids):
    tokens, depth = gradients.shape
    rank = proj_in.shape[1]
    chunks = max(n for n in (4, 2, 1) if depth % (n * LANES) == 0)
    hbm = pl.BlockSpec(memory_space=pltpu.HBM)
    vmem = pl.BlockSpec(memory_space=pltpu.VMEM)
    return pl.pallas_call(
        functools.partial(project_kernel, chunks),
        out_shape=(
            pltpu.VMEM((2 * rank, tokens), jnp.float32),
            pltpu.VMEM((8, tokens), jnp.float32),
            pltpu.VMEM((8, LANES), jnp.float32),
        ),
        in_specs=[hbm] * 5,
        out_specs=(vmem, vmem, vmem),
        scratch_shapes=[
            pltpu.VMEM((1, tokens), jnp.int32),
            pltpu.VMEM(activations.shape, jnp.bfloat16),
            pltpu.VMEM(proj_in.shape[::-1], jnp.bfloat16),
            pltpu.VMEM(gradients.shape, jnp.bfloat16),
            pltpu.VMEM(proj_out.shape[::-1], jnp.bfloat16),
            pltpu.SemaphoreType.DMA((3 + 2 * chunks,)),
        ],
        compiler_params=pltpu.CompilerParams(vmem_limit_bytes=VMEM_LIMIT),
    )(*kept(pltpu.HBM, doc_ids.reshape(1, tokens), activations, proj_in.T, gradients, proj_out.T))


def outer_kernel(part, other, mask, numbers, sums, tags, left):
    rank, tokens = left.shape
    left[...] = part[:rank, :] + other[:rank, :]
    right = part[rank:, :] + other[rank:, :]
    columns = [left[pl.ds(k, rank // 2, stride=2), :] for k in range(2)]
    weighted = jnp.concatenate(
        [jnp.concatenate([half * mask[s : s + 1, :] for half in columns], 1) for s in range(SLOTS)]
    )
    none = jnp.zeros_like(right)
    paired = jnp.concatenate(
        [jnp.concatenate([right, none], 1), jnp.concatenate([none, right], 1)]
    )
    found = lax.dot_general(
        weighted,
        paired,
        (((1,), (1,)), ((), ())),
        precision=lax.Precision.HIGHEST,
        preferred_element_type=jnp.float32,
    )
    largest = jnp.max(jnp.max(jnp.abs(found), 0, keepdims=True), 1, keepdims=True)
    power = jnp.floor(jnp.log2(jnp.maximum(largest, 1e-30)))
    sums[...] = found * jnp.exp2(TOP - power)
    rows = lax.broadcasted_iota(jnp.int32, numbers.shape, 0)
    tags[...] = numbers[...] * jnp.where(rows < 4, 1.0, jnp.broadcast_to(power, rows.shape))


def outer(part, other, mask, numbers):
    rank, tokens = part.shape[0] // 2, part.shape[1]
    vmem = pl.BlockSpec(memory_space=pltpu.VMEM)
    return pl.pallas_call(
        outer_kernel,
        out_shape=(
            pltpu.VMEM((SLOTS * rank // 2, 2 * rank), jnp.float32),
            pltpu.VMEM(numbers.shape, jnp.float32),
        ),
        in_specs=[vmem] * 4,
        out_specs=(vmem, vmem),
        scratch_shapes=[pltpu.VMEM((rank, tokens), jnp.float32)],
        compiler_params=pltpu.CompilerParams(vmem_limit_bytes=VMEM_LIMIT),
    )(*kept(pltpu.VMEM, part, other, mask, numbers))


def split(array):
    high = array.astype(jnp.bfloat16)
    return high, (array - high.astype(jnp.float32)).astype(jnp.bfloat16)


def precondition_kernel(own, other, upper, lower, out, pieces):
    depth = 2 * upper.shape[0]
    size = own.shape[0] - 8
    count = size * LANES // depth
    room = pieces.shape[0] // 2
    pieces[...] = jnp.zeros_like(pieces)
    for k in range(depth // LANES):
        for n, part in enumerate((own, other)):
            pieces[pl.ds(n * room, count), pl.ds(k * LANES, LANES)] = part[
                pl.ds(k, count, stride=depth // LANES), :
            ]
    step = 2 * LANES if depth % (4 * LANES) == 0 else LANES
    total = None
    for n in range(depth // step):
        high, low = split(pieces[:, pl.ds(n * step, step)])
        half, row = divmod(n * step, depth // 2)
        weights_high, weights_low = split((upper, lower)[half][pl.ds(row, step), :])
        first = jnp.dot(
            jnp.concatenate([high, low]), weights_high, preferred_element_type=jnp.float32
        )
        second = jnp.dot(high, weights_low, preferred_element_type=jnp.float32)
        term = first[: 2 * room] + (first[2 * room :] + second)
        total = term if total is None else total + term
    docs = lax.broadcasted_iota(jnp.int32, (out.shape[0], count), 0).astype(jnp.float32)
    result = None
    for n, part in enumerate((own, other)):
        rows = []
        for at in (0, 4):
            lanes = [
                jnp.concatenate(
                    [part[size + r : size + r + 1, :] for r in range(k, k + pl.cdiv(count // 2, LANES))], 1
                )[:, : count // 2]
                for k in (at, at + 2)
            ]
            rows.append(jnp.broadcast_to(jnp.concatenate(lanes, 1), docs.shape))
        lanes, powers = rows
        pick = jnp.where(lanes == docs, jnp.exp2(powers - TOP), 0.0)
        term = jnp.dot(
            pick,
            total[n * room : n * room + count],
            precision=lax.Precision.HIGHEST,
            preferred_element_type=jnp.float32,
        )
        result = term if result is None else result + term
    out[...] = result


def precondition(own, other, upper, lower, doc_count):
    vmem = pl.BlockSpec(memory_space=pltpu.VMEM)
    depth, width = 2 * upper.shape[0], upper.shape[1]
    count = (own.shape[0] - 8) * LANES // depth
    return pl.pallas_call(
        precondition_kernel,
        out_shape=pltpu.VMEM((doc_count, width), jnp.float32),
        in_specs=[vmem] * 4,
        out_specs=vmem,
        scratch_shapes=[pltpu.VMEM((2 * pl.cdiv(count, 8) * 8, depth), jnp.float32)],
        compiler_params=pltpu.CompilerParams(vmem_limit_bytes=VMEM_LIMIT),
    )(*kept(pltpu.VMEM, own, other, upper, lower))


def shards(activations, gradients, doc_ids, proj_in, proj_out, inverse, store_rows):
    ctx = lax.axis_size("ctx")
    rank = proj_in.shape[1]
    half = rank // lax.axis_size("col")
    doc_count = SLOTS * ctx // 2
    part, mask, numbers = project(activations, gradients, proj_in, proj_out, doc_ids)
    sums, tags = outer(part, swap_cores(part), mask, numbers)
    blocks, tags = sums.astype(jnp.float16), tags.astype(jnp.float16)
    for distance in far_distances():
        size = blocks.shape[0]
        other = swap_far(jnp.concatenate([blocks, tags]), distance)
        blocks = ordered(blocks, other[:size], distance)
        tags = tags + other[size:]
    rows = inverse.shape[0] // 2
    size = blocks.shape[0]
    other = swap_near(jnp.concatenate([blocks, tags]), 0)
    upper = fetch(inverse, 0, rows, tags.astype(jnp.float32))
    other, upper = lax.optimization_barrier((other, upper))
    blocks = jnp.concatenate([blocks, other[:size]])
    tags = tags + jnp.roll(other[size:], 2, 0)
    halves = blocks.reshape(-1, 2, half * rank // LANES, LANES)
    first = lax.axis_index("col") == 0
    own = jnp.where(first, halves[:, 0], halves[:, 1]).reshape(-1, LANES)
    others = jnp.where(first, halves[:, 1], halves[:, 0]).reshape(-1, LANES)
    payload = jnp.concatenate([own, tags]).astype(jnp.float32)
    other = swap_near(jnp.concatenate([others, tags]), 1)
    lower = fetch(inverse, rows, rows, payload)
    other, lower = lax.optimization_barrier((other, lower))
    partial_q = precondition(payload, other.astype(jnp.float32), upper, lower, doc_count)
    precond = (partial_q + swap_cores(partial_q)).astype(jnp.bfloat16)
    width = precond.shape[1]
    whole = precond.reshape(-1, min(width, LANES))
    for distance in far_distances():
        whole = ordered(whole, swap_far(whole, distance), distance)
    whole = jnp.stack([whole, swap_near(whole, 0)])
    (own, near), (next_one, farthest) = whole, swap_near(whole, 1)
    c, p = lax.axis_index("ctx"), lax.axis_index("col")
    single = near_distance(c, p, 0) == 1
    near, next_one = jnp.where(single, near, next_one), jnp.where(single, next_one, near)
    whole = jnp.stack([own, near, next_one, farthest])
    for bit in (1, 2):
        pairs = whole.reshape((2 // bit, 2, bit) + whole.shape[1:])
        whole = jnp.where((c & bit) != 0, pairs[:, ::-1], pairs).reshape(whole.shape)
    bits = len(far_distances())
    whole = whole.reshape((4,) + (2,) * bits + (doc_count, width))
    whole = whole.transpose((bits + 1,) + tuple(range(1, bits + 1))[::-1] + (0, bits + 2))
    whole = whole.reshape(doc_count, -1)
    return lax.dot_general(
        whole, store_rows, (((1,), (1,)), ((), ())), preferred_element_type=jnp.float32
    )


def solution(mesh):
    in_specs = (
        P(("groups", "ctx"), "col"),
        P(("groups", "ctx"), "col"),
        P(("groups", "ctx")),
        P("col", None),
        P("col", None),
        P("col", "ctx"),
        P(("groups", "ctx", "col"), None),
    )
    out_specs = P(None, ("groups", "ctx", "col"))
    return jax.shard_map(shards, mesh=mesh, in_specs=in_specs, out_specs=out_specs, check_vma=False)
```

```python
import functools

import jax
import jax.numpy as jnp
from jax import lax
from jax.experimental import pallas as pl
from jax.experimental.pallas import tpu as pltpu
from jax.sharding import PartitionSpec as P

SLOTS = 3
LANES = 128
TOP = 13.0
VMEM_LIMIT = 16 << 20


def far_distances():
    size = lax.axis_size("ctx")
    return [size >> step for step in range(1, size.bit_length() - 2)]


def near_distance(c, p, last):
    even = (c ^ (c >> 1) ^ p ^ last) & 1
    return 1 + even


def swap(block, partner):
    ctx, col = lax.axis_size("ctx"), lax.axis_size("col")
    route = []
    for c in range(ctx):
        for p in range(col):
            there, core = partner(c, p)
            route.append((c * col + p, there * col + core))
    return lax.ppermute(block, ("ctx", "col"), route)


def swap_cores(block):
    return swap(block, lambda c, p: (c, p ^ 1))


def swap_far(block, distance):
    return swap(block, lambda c, p: (c ^ distance, p ^ 1))


def swap_near(block, last):
    return swap(block, lambda c, p: (c ^ near_distance(c, p, last), p ^ 1))


def ordered(own, other, distance):
    upper = (lax.axis_index("ctx") & distance) != 0
    return jnp.where(upper, jnp.concatenate([other, own]), jnp.concatenate([own, other]))


def position():
    index, place = lax.axis_index("ctx"), 0
    for step, distance in enumerate(far_distances()):
        place = place + jnp.where((index & distance) != 0, 1 << step, 0)
    return place


def kept(space, *arrays):
    return [pltpu.with_memory_space_constraint(array, space) for array in arrays]


def split(array):
    high = array.astype(jnp.bfloat16)
    return high, (array - high.astype(jnp.float32)).astype(jnp.bfloat16)


def fetch_kernel(start, chunk, array, after, high, low, rows, sems):
    parts = [pl.ds(n * chunk, chunk) for n in range(rows.shape[0] // chunk)]
    copies = [
        pltpu.make_async_copy(array.at[pl.ds(start + n * chunk, chunk), :], rows.at[part, :], sems.at[n])
        for n, part in enumerate(parts)
    ]
    for copy in copies:
        copy.start()
    for copy, part in zip(copies, parts):
        copy.wait()
        high[part, :], low[part, :] = split(rows[part, :])


def fetch(array, start, rows, after):
    chunk = LANES
    vmem = pl.BlockSpec(memory_space=pltpu.VMEM)
    shape = (rows, array.shape[1])
    return pl.pallas_call(
        functools.partial(fetch_kernel, start, chunk),
        out_shape=(pltpu.VMEM(shape, jnp.bfloat16), pltpu.VMEM(shape, jnp.bfloat16)),
        in_specs=[pl.BlockSpec(memory_space=pltpu.HBM), vmem],
        out_specs=(vmem, vmem),
        scratch_shapes=[
            pltpu.VMEM(shape, array.dtype),
            pltpu.SemaphoreType.DMA((rows // chunk,)),
        ],
        compiler_params=pltpu.CompilerParams(vmem_limit_bytes=VMEM_LIMIT),
    )(*kept(pltpu.HBM, array), *kept(pltpu.VMEM, after))


def project_kernel(cuts, ids_hbm, act_hbm, pin_hbm, grad_hbm, pout_hbm, out, mask, numbers, ids, act, pin, grad, pout, sems):
    copies = []

    def copy(source, target):
        copies.append(pltpu.make_async_copy(source, target, sems.at[len(copies)]))
        copies[-1].start()
        return copies[-1]

    tokens = copy(ids_hbm, ids)
    left = (copy(pin_hbm, pin), copy(act_hbm, act))
    parts = [pl.ds(start, stop - start) for start, stop in zip(cuts, cuts[1:])]
    right = [
        (copy(pout_hbm.at[:, part], pout.at[:, part]), copy(grad_hbm.at[:, part], grad.at[:, part]))
        for part in parts
    ]
    tokens.wait()
    rows = lax.broadcasted_iota(jnp.int32, mask.shape, 0)
    first = jnp.broadcast_to(ids[:, :1], mask.shape)
    mask[...] = (jnp.broadcast_to(ids[...], mask.shape) - first == rows).astype(jnp.float32)
    shape = numbers.shape
    row = lax.broadcasted_iota(jnp.int32, shape, 0)
    place = row % 2 * LANES + lax.broadcasted_iota(jnp.int32, shape, 1) - SLOTS * position()
    first = jnp.broadcast_to(ids[:, :1], shape)
    value = jnp.where(row < 4, first + place, 1)
    owned = (place >= 0) & (place < SLOTS) & (row % 4 < 2)
    numbers[...] = jnp.where(owned, value, 0).astype(jnp.float32)
    rank = pin.shape[0]
    dims = (((1,), (1,)), ((), ()))
    for piece in left:
        piece.wait()
    out[:rank, :] = lax.dot_general(pin[...], act[...], dims, preferred_element_type=jnp.float32)
    total = None
    for part, pair in zip(parts, right):
        for piece in pair:
            piece.wait()
        term = lax.dot_general(pout[:, part], grad[:, part], dims, preferred_element_type=jnp.float32)
        total = term if total is None else total + term
    out[rank:, :] = total


def project(activations, gradients, proj_in, proj_out, doc_ids):
    tokens, depth = gradients.shape
    rank = proj_in.shape[1]
    cuts = [depth * n // 14 // LANES * LANES for n in (0, 5, 9, 12, 13, 14)]
    hbm = pl.BlockSpec(memory_space=pltpu.HBM)
    vmem = pl.BlockSpec(memory_space=pltpu.VMEM)
    return pl.pallas_call(
        functools.partial(project_kernel, cuts),
        out_shape=(
            pltpu.VMEM((2 * rank, tokens), jnp.float32),
            pltpu.VMEM((8, tokens), jnp.float32),
            pltpu.VMEM((8, LANES), jnp.float32),
        ),
        in_specs=[hbm] * 5,
        out_specs=(vmem, vmem, vmem),
        scratch_shapes=[
            pltpu.VMEM((1, tokens), jnp.int32),
            pltpu.VMEM(activations.shape, jnp.bfloat16),
            pltpu.VMEM(proj_in.shape[::-1], jnp.bfloat16),
            pltpu.VMEM(gradients.shape, jnp.bfloat16),
            pltpu.VMEM(proj_out.shape[::-1], jnp.bfloat16),
            pltpu.SemaphoreType.DMA((1 + 2 * len(cuts),)),
        ],
        compiler_params=pltpu.CompilerParams(vmem_limit_bytes=VMEM_LIMIT),
    )(*kept(pltpu.HBM, doc_ids.reshape(1, tokens), activations, proj_in.T, gradients, proj_out.T))


def outer_kernel(part, other, mask, numbers, sums, tags, left):
    rank, tokens = left.shape
    left[...] = part[:rank, :] + other[:rank, :]
    right = part[rank:, :] + other[rank:, :]
    columns = [left[pl.ds(k, rank // 2, stride=2), :] for k in range(2)]
    weighted = jnp.concatenate(
        [jnp.concatenate([half * mask[s : s + 1, :] for half in columns], 1) for s in range(SLOTS)]
    )
    none = jnp.zeros_like(right)
    paired = jnp.concatenate(
        [jnp.concatenate([right, none], 1), jnp.concatenate([none, right], 1)]
    )
    found = lax.dot_general(
        weighted,
        paired,
        (((1,), (1,)), ((), ())),
        precision=lax.Precision.HIGHEST,
        preferred_element_type=jnp.float32,
    )
    largest = jnp.max(jnp.max(jnp.abs(found), 0, keepdims=True), 1, keepdims=True)
    power = jnp.floor(jnp.log2(jnp.maximum(largest, 1e-30)))
    sums[...] = found * jnp.exp2(TOP - power)
    rows = lax.broadcasted_iota(jnp.int32, numbers.shape, 0)
    tags[...] = numbers[...] * jnp.where(rows < 4, 1.0, jnp.broadcast_to(power, rows.shape))


def outer(part, other, mask, numbers):
    rank, tokens = part.shape[0] // 2, part.shape[1]
    vmem = pl.BlockSpec(memory_space=pltpu.VMEM)
    return pl.pallas_call(
        outer_kernel,
        out_shape=(
            pltpu.VMEM((SLOTS * rank // 2, 2 * rank), jnp.float32),
            pltpu.VMEM(numbers.shape, jnp.float32),
        ),
        in_specs=[vmem] * 4,
        out_specs=(vmem, vmem),
        scratch_shapes=[pltpu.VMEM((rank, tokens), jnp.float32)],
        compiler_params=pltpu.CompilerParams(vmem_limit_bytes=VMEM_LIMIT),
    )(*kept(pltpu.VMEM, part, other, mask, numbers))


def precondition_kernel(windows, own, other, *refs):
    highs, lows, (out, pieces) = refs[:windows], refs[windows : 2 * windows], refs[2 * windows :]
    depth = pieces.shape[1]
    size = own.shape[0] - 8
    count = size * LANES // depth
    room = pieces.shape[0] // 2
    pieces[...] = jnp.zeros_like(pieces)
    for k in range(depth // LANES):
        for n, part in enumerate((own, other)):
            pieces[pl.ds(n * room, count), pl.ds(k * LANES, LANES)] = part[
                pl.ds(k, count, stride=depth // LANES), :
            ]
    first, second, at = None, None, 0
    for weights_high, weights_low in zip(highs, lows):
        rows = weights_high.shape[0]
        high, low = split(pieces[:, pl.ds(at, rows)])
        term = jnp.dot(
            jnp.concatenate([high, low]), weights_high[...], preferred_element_type=jnp.float32
        )
        first = term if first is None else first + term
        term = jnp.dot(high, weights_low[...], preferred_element_type=jnp.float32)
        second = term if second is None else second + term
        at += rows
    total = first[: 2 * room] + (first[2 * room :] + second)
    docs = lax.broadcasted_iota(jnp.int32, (out.shape[0], count), 0).astype(jnp.float32)
    result = None
    for n, part in enumerate((own, other)):
        rows = []
        for at in (0, 4):
            lanes = [
                jnp.concatenate(
                    [part[size + r : size + r + 1, :] for r in range(k, k + pl.cdiv(count // 2, LANES))], 1
                )[:, : count // 2]
                for k in (at, at + 2)
            ]
            rows.append(jnp.broadcast_to(jnp.concatenate(lanes, 1), docs.shape))
        lanes, powers = rows
        pick = jnp.where(lanes == docs, jnp.exp2(powers - TOP), 0.0)
        term = jnp.dot(
            pick,
            total[n * room : n * room + count],
            precision=lax.Precision.HIGHEST,
            preferred_element_type=jnp.float32,
        )
        result = term if result is None else result + term
    out[...] = result


def precondition(own, other, highs, lows, doc_count):
    vmem = pl.BlockSpec(memory_space=pltpu.VMEM)
    depth, width = sum(high.shape[0] for high in highs), highs[0].shape[1]
    count = (own.shape[0] - 8) * LANES // depth
    return pl.pallas_call(
        functools.partial(precondition_kernel, len(highs)),
        out_shape=pltpu.VMEM((doc_count, width), jnp.float32),
        in_specs=[vmem] * (2 + 2 * len(highs)),
        out_specs=vmem,
        scratch_shapes=[pltpu.VMEM((2 * pl.cdiv(count, 8) * 8, depth), jnp.float32)],
        compiler_params=pltpu.CompilerParams(vmem_limit_bytes=VMEM_LIMIT),
    )(*kept(pltpu.VMEM, own, other, *highs, *lows))


def load_kernel(source, after, target, sem):
    copy = pltpu.make_async_copy(source, target, sem)
    copy.start()
    copy.wait()


def load(array, after):
    vmem = pl.BlockSpec(memory_space=pltpu.VMEM)
    return pl.pallas_call(
        load_kernel,
        out_shape=pltpu.VMEM(array.shape, array.dtype),
        in_specs=[pl.BlockSpec(memory_space=pltpu.HBM), vmem],
        out_specs=vmem,
        scratch_shapes=[pltpu.SemaphoreType.DMA],
        compiler_params=pltpu.CompilerParams(vmem_limit_bytes=VMEM_LIMIT),
    )(*kept(pltpu.HBM, array), *kept(pltpu.VMEM, after))


def score_kernel(width, mine, theirs, store, out, products):
    pieces = width // LANES
    count = store.shape[0]
    rows = out.shape[0] * pieces
    chunk = mine.shape[0] // 2
    held = chunk // rows
    bits = held.bit_length() - 1
    c, p = lax.axis_index("ctx"), lax.axis_index("col")
    first, second = (near_distance(c, p, last) for last in (0, 1))
    total = None
    for part, n, offset in ((mine, 0, 0), (mine, 1, first), (theirs, 0, second), (theirs, 1, 3)):
        low = (c & 3) ^ offset
        blocks, columns = [], [[] for _ in range(pieces)]
        for place in range(held):
            high = sum(((place >> k) & 1) << (bits - 1 - k) for k in range(bits))
            start = (high * 4 + low) * width
            blocks.append(part[pl.ds(n * chunk + place * rows, rows), :])
            for k in range(pieces):
                at = pl.multiple_of(start + k * LANES, LANES)
                columns[k].append(store[:, pl.ds(at, LANES)])
        left = jnp.concatenate(blocks, 1)
        right = jnp.concatenate([jnp.concatenate(column, 1) for column in columns])
        term = lax.dot_general(
            left, right, (((1,), (1,)), ((), ())), preferred_element_type=jnp.float32
        )
        total = term if total is None else total + term
    for n in range(products.shape[0] // rows):
        products[pl.ds(n * rows, rows), :] = total[:, n * LANES : (n + 1) * LANES]
    result = None
    for k in range(pieces):
        slab, lane = divmod(k * count, LANES)
        lines = products[pl.ds(slab * rows + k, rows // pieces, stride=pieces), :]
        term = lines[:, lane : lane + count]
        result = term if result is None else result + term
    out[...] = result


def score(mine, theirs, store, width, doc_count):
    vmem = pl.BlockSpec(memory_space=pltpu.VMEM)
    pieces = width // LANES
    return pl.pallas_call(
        functools.partial(score_kernel, width),
        out_shape=jax.ShapeDtypeStruct((doc_count, store.shape[0]), jnp.float32),
        in_specs=[vmem] * 3,
        out_specs=vmem,
        scratch_shapes=[
            pltpu.VMEM((doc_count * pieces * (pieces * store.shape[0] // LANES), LANES), jnp.float32)
        ],
        compiler_params=pltpu.CompilerParams(vmem_limit_bytes=VMEM_LIMIT),
    )(*kept(pltpu.VMEM, mine, theirs, store))


def shards(activations, gradients, doc_ids, proj_in, proj_out, inverse, store_rows):
    ctx = lax.axis_size("ctx")
    rank = proj_in.shape[1]
    half = rank // lax.axis_size("col")
    doc_count = SLOTS * ctx // 2
    part, mask, numbers = project(activations, gradients, proj_in, proj_out, doc_ids)
    sums, tags = outer(part, swap_cores(part), mask, numbers)
    blocks, tags = sums.astype(jnp.float16), tags.astype(jnp.float16)
    depth = inverse.shape[0]
    cuts = [0] + [depth * k // 8 // LANES * LANES for k in ((2, 5) if far_distances() else (4,))] + [depth]
    highs, lows = [], []

    def beside(exchange, payload, ready):
        other, at = exchange(payload), len(highs)
        pair = fetch(inverse, cuts[at], cuts[at + 1] - cuts[at], ready)
        other, high, low = lax.optimization_barrier((other, *pair))
        highs.append(high)
        lows.append(low)
        return other

    for distance in far_distances():
        size = blocks.shape[0]
        exchange = functools.partial(swap_far, distance=distance)
        payload = jnp.concatenate([blocks, tags])
        if distance == far_distances()[-1]:
            other = beside(exchange, payload, tags.astype(jnp.float32))
        else:
            other = exchange(payload)
        blocks = ordered(blocks, other[:size], distance)
        tags = tags + other[size:]
    size = blocks.shape[0]
    payload = jnp.concatenate([blocks, tags])
    other = beside(functools.partial(swap_near, last=0), payload, tags.astype(jnp.float32))
    blocks = jnp.concatenate([blocks, other[:size]])
    tags = tags + jnp.roll(other[size:], 2, 0)
    halves = blocks.reshape(-1, 2, half * rank // LANES, LANES)
    first = lax.axis_index("col") == 0
    own = jnp.where(first, halves[:, 0], halves[:, 1]).reshape(-1, LANES)
    others = jnp.where(first, halves[:, 1], halves[:, 0]).reshape(-1, LANES)
    own = jnp.concatenate([own, tags]).astype(jnp.float32)
    other = beside(functools.partial(swap_near, last=1), jnp.concatenate([others, tags]), own)
    partial_q = precondition(own, other.astype(jnp.float32), highs, lows, doc_count)
    precond = (partial_q + swap_cores(partial_q)).astype(jnp.bfloat16)
    width = precond.shape[1]
    whole = precond.reshape(-1, min(width, LANES))
    count = store_rows.shape[0]
    direct = width % LANES == 0 and LANES % count == 0 and width * count % LANES**2 == 0
    if direct:
        store = load(store_rows, whole)
    for step, distance in enumerate(far_distances()):
        other = swap_far(whole, distance)
        if direct and step == 0:
            other, store = lax.optimization_barrier((other, store))
        whole = ordered(whole, other, distance)
    whole = jnp.concatenate([whole, swap_near(whole, 0)])
    others = swap_near(whole, 1)
    if direct:
        return score(whole, others, store, width, doc_count)
    (own, near), (next_one, farthest) = (x.reshape(2, -1, x.shape[1]) for x in (whole, others))
    c, p = lax.axis_index("ctx"), lax.axis_index("col")
    single = near_distance(c, p, 0) == 1
    near, next_one = jnp.where(single, near, next_one), jnp.where(single, next_one, near)
    whole = jnp.stack([own, near, next_one, farthest])
    for bit in (1, 2):
        pairs = whole.reshape((2 // bit, 2, bit) + whole.shape[1:])
        whole = jnp.where((c & bit) != 0, pairs[:, ::-1], pairs).reshape(whole.shape)
    bits = len(far_distances())
    whole = whole.reshape((4,) + (2,) * bits + (doc_count, width))
    whole = whole.transpose((bits + 1,) + tuple(range(1, bits + 1))[::-1] + (0, bits + 2))
    whole = whole.reshape(doc_count, -1)
    return lax.dot_general(
        whole, store_rows, (((1,), (1,)), ((), ())), preferred_element_type=jnp.float32
    )


def solution(mesh):
    in_specs = (
        P(("groups", "ctx"), "col"),
        P(("groups", "ctx"), "col"),
        P(("groups", "ctx")),
        P("col", None),
        P("col", None),
        P("col", "ctx"),
        P(("groups", "ctx", "col"), None),
    )
    out_specs = P(None, ("groups", "ctx", "col"))
    return jax.shard_map(shards, mesh=mesh, in_specs=in_specs, out_specs=out_specs, check_vma=False)
```

```python
import functools

import jax
import jax.numpy as jnp
from jax import lax
from jax.experimental import pallas as pl
from jax.experimental.pallas import tpu as pltpu
from jax.sharding import PartitionSpec as P

SLOTS = 3
LANES = 128
TOP = 13.0
VMEM_LIMIT = 16 << 20


def far_distances():
    size = lax.axis_size("ctx")
    return [size >> step for step in range(1, size.bit_length() - 2)]


def near_distance(c, p, last):
    even = (c ^ (c >> 1) ^ p ^ last) & 1
    return 1 + even


def swap(block, partner):
    ctx, col = lax.axis_size("ctx"), lax.axis_size("col")
    route = []
    for c in range(ctx):
        for p in range(col):
            there, core = partner(c, p)
            route.append((c * col + p, there * col + core))
    return lax.ppermute(block, ("ctx", "col"), route)


def swap_cores(block):
    return swap(block, lambda c, p: (c, p ^ 1))


def swap_far(block, distance):
    return swap(block, lambda c, p: (c ^ distance, p ^ 1))


def swap_near(block, last):
    return swap(block, lambda c, p: (c ^ near_distance(c, p, last), p ^ 1))


def ordered(own, other, distance):
    upper = (lax.axis_index("ctx") & distance) != 0
    return jnp.where(upper, jnp.concatenate([other, own]), jnp.concatenate([own, other]))


def position():
    index, place = lax.axis_index("ctx"), 0
    for step, distance in enumerate(far_distances()):
        place = place + jnp.where((index & distance) != 0, 1 << step, 0)
    return place


def kept(space, *arrays):
    return [pltpu.with_memory_space_constraint(array, space) for array in arrays]


def split(array):
    high = array.astype(jnp.bfloat16)
    return high, (array - high.astype(jnp.float32)).astype(jnp.bfloat16)


def fetch_kernel(start, chunk, array, after, high, low, rows, sems):
    parts = [pl.ds(n * chunk, chunk) for n in range(rows.shape[0] // chunk)]
    copies = [
        pltpu.make_async_copy(array.at[pl.ds(start + n * chunk, chunk), :], rows.at[part, :], sems.at[n])
        for n, part in enumerate(parts)
    ]
    for copy in copies:
        copy.start()
    for copy, part in zip(copies, parts):
        copy.wait()
        high[part, :], low[part, :] = split(rows[part, :])


def fetch(array, start, rows, after):
    chunk = LANES
    vmem = pl.BlockSpec(memory_space=pltpu.VMEM)
    shape = (rows, array.shape[1])
    return pl.pallas_call(
        functools.partial(fetch_kernel, start, chunk),
        out_shape=(pltpu.VMEM(shape, jnp.bfloat16), pltpu.VMEM(shape, jnp.bfloat16)),
        in_specs=[pl.BlockSpec(memory_space=pltpu.HBM), vmem],
        out_specs=(vmem, vmem),
        scratch_shapes=[
            pltpu.VMEM(shape, array.dtype),
            pltpu.SemaphoreType.DMA((rows // chunk,)),
        ],
        compiler_params=pltpu.CompilerParams(vmem_limit_bytes=VMEM_LIMIT),
    )(*kept(pltpu.HBM, array), *kept(pltpu.VMEM, after))


def project_kernel(cuts, ids_hbm, act_hbm, pin_hbm, grad_hbm, pout_hbm, out, mask, numbers, ids, act, pin, grad, pout, sems):
    copies = []

    def copy(source, target):
        copies.append(pltpu.make_async_copy(source, target, sems.at[len(copies)]))
        copies[-1].start()
        return copies[-1]

    tokens = copy(ids_hbm, ids)
    left = (copy(pin_hbm, pin), copy(act_hbm, act))
    parts = [pl.ds(start, stop - start) for start, stop in zip(cuts, cuts[1:])]
    right = [
        (copy(pout_hbm.at[:, part], pout.at[:, part]), copy(grad_hbm.at[:, part], grad.at[:, part]))
        for part in parts
    ]
    tokens.wait()
    rows = lax.broadcasted_iota(jnp.int32, mask.shape, 0)
    first = jnp.broadcast_to(ids[:, :1], mask.shape)
    mask[...] = (jnp.broadcast_to(ids[...], mask.shape) - first == rows).astype(jnp.float32)
    shape = numbers.shape
    row = lax.broadcasted_iota(jnp.int32, shape, 0)
    place = row % 2 * LANES + lax.broadcasted_iota(jnp.int32, shape, 1) - SLOTS * position()
    first = jnp.broadcast_to(ids[:, :1], shape)
    value = jnp.where(row < 4, first + place, 1)
    owned = (place >= 0) & (place < SLOTS) & (row % 4 < 2)
    numbers[...] = jnp.where(owned, value, 0).astype(jnp.float32)
    rank = pin.shape[0]
    dims = (((1,), (1,)), ((), ()))
    for piece in left:
        piece.wait()
    out[:rank, :] = lax.dot_general(pin[...], act[...], dims, preferred_element_type=jnp.float32)
    total = None
    for part, pair in zip(parts, right):
        for piece in pair:
            piece.wait()
        term = lax.dot_general(pout[:, part], grad[:, part], dims, preferred_element_type=jnp.float32)
        total = term if total is None else total + term
    out[rank:, :] = total


def project(activations, gradients, proj_in, proj_out, doc_ids):
    tokens, depth = gradients.shape
    rank = proj_in.shape[1]
    cuts = sorted({depth * n // 14 // LANES * LANES for n in (0, 5, 9, 12, 13)} | {depth})
    hbm = pl.BlockSpec(memory_space=pltpu.HBM)
    vmem = pl.BlockSpec(memory_space=pltpu.VMEM)
    return pl.pallas_call(
        functools.partial(project_kernel, cuts),
        out_shape=(
            pltpu.VMEM((2 * rank, tokens), jnp.float32),
            pltpu.VMEM((8, tokens), jnp.float32),
            pltpu.VMEM((8, LANES), jnp.float32),
        ),
        in_specs=[hbm] * 5,
        out_specs=(vmem, vmem, vmem),
        scratch_shapes=[
            pltpu.VMEM((1, tokens), jnp.int32),
            pltpu.VMEM(activations.shape, jnp.bfloat16),
            pltpu.VMEM(proj_in.shape[::-1], jnp.bfloat16),
            pltpu.VMEM(gradients.shape, jnp.bfloat16),
            pltpu.VMEM(proj_out.shape[::-1], jnp.bfloat16),
            pltpu.SemaphoreType.DMA((1 + 2 * len(cuts),)),
        ],
        compiler_params=pltpu.CompilerParams(vmem_limit_bytes=VMEM_LIMIT),
    )(*kept(pltpu.HBM, doc_ids.reshape(1, tokens), activations, proj_in.T, gradients, proj_out.T))


def outer_kernel(part, other, mask, numbers, sums, tags, left):
    rank, tokens = left.shape
    left[...] = part[:rank, :] + other[:rank, :]
    right = part[rank:, :] + other[rank:, :]
    columns = [left[pl.ds(k, rank // 2, stride=2), :] for k in range(2)]
    weighted = jnp.concatenate(
        [jnp.concatenate([half * mask[s : s + 1, :] for half in columns], 1) for s in range(SLOTS)]
    )
    none = jnp.zeros_like(right)
    paired = jnp.concatenate(
        [jnp.concatenate([right, none], 1), jnp.concatenate([none, right], 1)]
    )
    found = lax.dot_general(
        weighted,
        paired,
        (((1,), (1,)), ((), ())),
        precision=lax.Precision.HIGHEST,
        preferred_element_type=jnp.float32,
    )
    largest = jnp.max(jnp.max(jnp.abs(found), 0, keepdims=True), 1, keepdims=True)
    power = jnp.floor(jnp.log2(jnp.maximum(largest, 1e-30)))
    sums[...] = found * jnp.exp2(TOP - power)
    rows = lax.broadcasted_iota(jnp.int32, numbers.shape, 0)
    tags[...] = numbers[...] * jnp.where(rows < 4, 1.0, jnp.broadcast_to(power, rows.shape))


def outer(part, other, mask, numbers):
    rank, tokens = part.shape[0] // 2, part.shape[1]
    vmem = pl.BlockSpec(memory_space=pltpu.VMEM)
    return pl.pallas_call(
        outer_kernel,
        out_shape=(
            pltpu.VMEM((SLOTS * rank // 2, 2 * rank), jnp.float32),
            pltpu.VMEM(numbers.shape, jnp.float32),
        ),
        in_specs=[vmem] * 4,
        out_specs=(vmem, vmem),
        scratch_shapes=[pltpu.VMEM((rank, tokens), jnp.float32)],
        compiler_params=pltpu.CompilerParams(vmem_limit_bytes=VMEM_LIMIT),
    )(*kept(pltpu.VMEM, part, other, mask, numbers))


def precondition_kernel(windows, own, other, *refs):
    highs, lows, (out, pieces) = refs[:windows], refs[windows : 2 * windows], refs[2 * windows :]
    depth = pieces.shape[1]
    size = own.shape[0] - 8
    count = size * LANES // depth
    room = pieces.shape[0] // 2
    pieces[...] = jnp.zeros_like(pieces)
    for k in range(depth // LANES):
        for n, part in enumerate((own, other)):
            pieces[pl.ds(n * room, count), pl.ds(k * LANES, LANES)] = part[
                pl.ds(k, count, stride=depth // LANES), :
            ]
    first, second, at = None, None, 0
    for weights_high, weights_low in zip(highs, lows):
        rows = weights_high.shape[0]
        high, low = split(pieces[:, pl.ds(at, rows)])
        term = jnp.dot(
            jnp.concatenate([high, low]), weights_high[...], preferred_element_type=jnp.float32
        )
        first = term if first is None else first + term
        term = jnp.dot(high, weights_low[...], preferred_element_type=jnp.float32)
        second = term if second is None else second + term
        at += rows
    total = first[: 2 * room] + (first[2 * room :] + second)
    docs = lax.broadcasted_iota(jnp.int32, (out.shape[0], count), 0).astype(jnp.float32)
    result = None
    for n, part in enumerate((own, other)):
        rows = []
        for at in (0, 4):
            lanes = [
                jnp.concatenate(
                    [part[size + r : size + r + 1, :] for r in range(k, k + pl.cdiv(count // 2, LANES))], 1
                )[:, : count // 2]
                for k in (at, at + 2)
            ]
            rows.append(jnp.broadcast_to(jnp.concatenate(lanes, 1), docs.shape))
        lanes, powers = rows
        pick = jnp.where(lanes == docs, jnp.exp2(powers - TOP), 0.0)
        term = jnp.dot(
            pick,
            total[n * room : n * room + count],
            precision=lax.Precision.HIGHEST,
            preferred_element_type=jnp.float32,
        )
        result = term if result is None else result + term
    out[...] = result


def precondition(own, other, highs, lows, doc_count):
    vmem = pl.BlockSpec(memory_space=pltpu.VMEM)
    depth, width = sum(high.shape[0] for high in highs), highs[0].shape[1]
    count = (own.shape[0] - 8) * LANES // depth
    return pl.pallas_call(
        functools.partial(precondition_kernel, len(highs)),
        out_shape=pltpu.VMEM((doc_count, width), jnp.float32),
        in_specs=[vmem] * (2 + 2 * len(highs)),
        out_specs=vmem,
        scratch_shapes=[pltpu.VMEM((2 * pl.cdiv(count, 8) * 8, depth), jnp.float32)],
        compiler_params=pltpu.CompilerParams(vmem_limit_bytes=VMEM_LIMIT),
    )(*kept(pltpu.VMEM, own, other, *highs, *lows))


def load_kernel(source, after, target, sem):
    copy = pltpu.make_async_copy(source, target, sem)
    copy.start()
    copy.wait()


def load(array, after):
    vmem = pl.BlockSpec(memory_space=pltpu.VMEM)
    return pl.pallas_call(
        load_kernel,
        out_shape=pltpu.VMEM(array.shape, array.dtype),
        in_specs=[pl.BlockSpec(memory_space=pltpu.HBM), vmem],
        out_specs=vmem,
        scratch_shapes=[pltpu.SemaphoreType.DMA],
        compiler_params=pltpu.CompilerParams(vmem_limit_bytes=VMEM_LIMIT),
    )(*kept(pltpu.HBM, array), *kept(pltpu.VMEM, after))


def column_products(width, rows, held, pair, offsets, store):
    pieces = width // LANES
    bits = held.bit_length() - 1
    total = None
    for n, offset in enumerate(offsets):
        low = (lax.axis_index("ctx") & 3) ^ offset
        blocks, columns = [], [[] for _ in range(pieces)]
        for place in range(held):
            high = sum(((place >> k) & 1) << (bits - 1 - k) for k in range(bits))
            blocks.append(pair[pl.ds((n * held + place) * rows, rows), :])
            for k in range(pieces):
                at = pl.multiple_of((high * 4 + low) * width + k * LANES, LANES)
                columns[k].append(store[:, pl.ds(at, LANES)])
        left = jnp.concatenate(blocks, 1)
        right = jnp.concatenate([jnp.concatenate(column, 1) for column in columns])
        term = lax.dot_general(
            left, right, (((1,), (1,)), ((), ())), preferred_element_type=jnp.float32
        )
        total = term if total is None else total + term
    return total


def held_kernel(width, mine, store, out):
    rows = out.shape[0]
    first = near_distance(lax.axis_index("ctx"), lax.axis_index("col"), 0)
    held = mine.shape[0] // (2 * rows)
    out[...] = column_products(width, rows, held, mine, (0, first), store)


def score_kernel(width, known, theirs, store, out, products):
    rows, count = known.shape[0], store.shape[0]
    pieces = width // LANES
    second = near_distance(lax.axis_index("ctx"), lax.axis_index("col"), 1)
    held = theirs.shape[0] // (2 * rows)
    total = known[...] + column_products(width, rows, held, theirs, (second, 3), store)
    for n in range(products.shape[0] // rows):
        products[pl.ds(n * rows, rows), :] = total[:, n * LANES : (n + 1) * LANES]
    result = None
    for k in range(pieces):
        slab, lane = divmod(k * count, LANES)
        lines = products[pl.ds(slab * rows + k, rows // pieces, stride=pieces), :]
        term = lines[:, lane : lane + count]
        result = term if result is None else result + term
    out[...] = result


def score_held(mine, store, width, doc_count):
    vmem = pl.BlockSpec(memory_space=pltpu.VMEM)
    pieces = width // LANES
    return pl.pallas_call(
        functools.partial(held_kernel, width),
        out_shape=pltpu.VMEM((doc_count * pieces, pieces * store.shape[0]), jnp.float32),
        in_specs=[vmem] * 2,
        out_specs=vmem,
        compiler_params=pltpu.CompilerParams(vmem_limit_bytes=VMEM_LIMIT),
    )(*kept(pltpu.VMEM, mine, store))


def score(known, theirs, store, width, doc_count):
    vmem = pl.BlockSpec(memory_space=pltpu.VMEM)
    slabs = width // LANES * store.shape[0] // LANES
    return pl.pallas_call(
        functools.partial(score_kernel, width),
        out_shape=jax.ShapeDtypeStruct((doc_count, store.shape[0]), jnp.float32),
        in_specs=[vmem] * 3,
        out_specs=vmem,
        scratch_shapes=[pltpu.VMEM((slabs * known.shape[0], LANES), jnp.float32)],
        compiler_params=pltpu.CompilerParams(vmem_limit_bytes=VMEM_LIMIT),
    )(*kept(pltpu.VMEM, known, theirs, store))


def shards(activations, gradients, doc_ids, proj_in, proj_out, inverse, store_rows):
    ctx = lax.axis_size("ctx")
    rank = proj_in.shape[1]
    half = rank // lax.axis_size("col")
    doc_count = SLOTS * ctx // 2
    part, mask, numbers = project(activations, gradients, proj_in, proj_out, doc_ids)
    sums, tags = outer(part, swap_cores(part), mask, numbers)
    blocks, tags = sums.astype(jnp.float16), tags.astype(jnp.float16)
    depth = inverse.shape[0]
    cuts = [0] + [depth * k // 8 // LANES * LANES for k in ((2, 5) if far_distances() else (4,))] + [depth]
    highs, lows = [], []

    def beside(exchange, payload, ready):
        other, at = exchange(payload), len(highs)
        pair = fetch(inverse, cuts[at], cuts[at + 1] - cuts[at], ready)
        other, high, low = lax.optimization_barrier((other, *pair))
        highs.append(high)
        lows.append(low)
        return other

    for distance in far_distances():
        size = blocks.shape[0]
        exchange = functools.partial(swap_far, distance=distance)
        payload = jnp.concatenate([blocks, tags])
        if distance == far_distances()[-1]:
            other = beside(exchange, payload, tags.astype(jnp.float32))
        else:
            other = exchange(payload)
        blocks = ordered(blocks, other[:size], distance)
        tags = tags + other[size:]
    size = blocks.shape[0]
    payload = jnp.concatenate([blocks, tags])
    other = beside(functools.partial(swap_near, last=0), payload, tags.astype(jnp.float32))
    blocks = jnp.concatenate([blocks, other[:size]])
    tags = tags + jnp.roll(other[size:], 2, 0)
    halves = blocks.reshape(-1, 2, half * rank // LANES, LANES)
    first = lax.axis_index("col") == 0
    own = jnp.where(first, halves[:, 0], halves[:, 1]).reshape(-1, LANES)
    others = jnp.where(first, halves[:, 1], halves[:, 0]).reshape(-1, LANES)
    own = jnp.concatenate([own, tags]).astype(jnp.float32)
    other = beside(functools.partial(swap_near, last=1), jnp.concatenate([others, tags]), own)
    partial_q = precondition(own, other.astype(jnp.float32), highs, lows, doc_count)
    precond = (partial_q + swap_cores(partial_q)).astype(jnp.bfloat16)
    width = precond.shape[1]
    whole = precond.reshape(-1, min(width, LANES))
    count = store_rows.shape[0]
    direct = width % LANES == 0 and LANES % count == 0 and width * count % LANES**2 == 0
    if direct:
        store = load(store_rows, whole)
    for step, distance in enumerate(far_distances()):
        other = swap_far(whole, distance)
        if direct and step == 0:
            other, store = lax.optimization_barrier((other, store))
        whole = ordered(whole, other, distance)
    whole = jnp.concatenate([whole, swap_near(whole, 0)])
    others = swap_near(whole, 1)
    if direct:
        known = score_held(whole, store, width, doc_count)
        others, known = lax.optimization_barrier((others, known))
        return score(known, others, store, width, doc_count)
    (own, near), (next_one, farthest) = (x.reshape(2, -1, x.shape[1]) for x in (whole, others))
    c, p = lax.axis_index("ctx"), lax.axis_index("col")
    single = near_distance(c, p, 0) == 1
    near, next_one = jnp.where(single, near, next_one), jnp.where(single, next_one, near)
    whole = jnp.stack([own, near, next_one, farthest])
    for bit in (1, 2):
        pairs = whole.reshape((2 // bit, 2, bit) + whole.shape[1:])
        whole = jnp.where((c & bit) != 0, pairs[:, ::-1], pairs).reshape(whole.shape)
    bits = len(far_distances())
    whole = whole.reshape((4,) + (2,) * bits + (doc_count, width))
    whole = whole.transpose((bits + 1,) + tuple(range(1, bits + 1))[::-1] + (0, bits + 2))
    whole = whole.reshape(doc_count, -1)
    return lax.dot_general(
        whole, store_rows, (((1,), (1,)), ((), ())), preferred_element_type=jnp.float32
    )


def solution(mesh):
    in_specs = (
        P(("groups", "ctx"), "col"),
        P(("groups", "ctx"), "col"),
        P(("groups", "ctx")),
        P("col", None),
        P("col", None),
        P("col", "ctx"),
        P(("groups", "ctx", "col"), None),
    )
    out_specs = P(None, ("groups", "ctx", "col"))
    return jax.shard_map(shards, mesh=mesh, in_specs=in_specs, out_specs=out_specs, check_vma=False)
```

```python
import functools

import jax
import jax.numpy as jnp
from jax import lax
from jax.experimental import pallas as pl
from jax.experimental.pallas import tpu as pltpu
from jax.sharding import PartitionSpec as P

SLOTS = 3
LANES = 128
TOP = 13.0
VMEM_LIMIT = 16 << 20


def far_distances():
    size = lax.axis_size("ctx")
    return [size >> step for step in range(1, size.bit_length() - 2)]


def near_distance(c, p, last):
    even = (c ^ (c >> 1) ^ p ^ last) & 1
    return 1 + even


def swap(block, partner):
    ctx, col = lax.axis_size("ctx"), lax.axis_size("col")
    route = []
    for c in range(ctx):
        for p in range(col):
            there, core = partner(c, p)
            route.append((c * col + p, there * col + core))
    return lax.ppermute(block, ("ctx", "col"), route)


def swap_cores(block):
    return swap(block, lambda c, p: (c, p ^ 1))


def swap_far(block, distance):
    return swap(block, lambda c, p: (c ^ distance, p ^ 1))


def swap_near(block, last):
    return swap(block, lambda c, p: (c ^ near_distance(c, p, last), p ^ 1))


def ordered(own, other, distance):
    upper = (lax.axis_index("ctx") & distance) != 0
    return jnp.where(upper, jnp.concatenate([other, own]), jnp.concatenate([own, other]))


def position():
    index, place = lax.axis_index("ctx"), 0
    for step, distance in enumerate(far_distances()):
        place = place + jnp.where((index & distance) != 0, 1 << step, 0)
    return place


def kept(space, *arrays):
    return [pltpu.with_memory_space_constraint(array, space) for array in arrays]


def split(array):
    high = array.astype(jnp.bfloat16)
    return high, (array - high.astype(jnp.float32)).astype(jnp.bfloat16)


def fetch_kernel(start, chunk, array, after, high, low, rows, sems):
    parts = [pl.ds(n * chunk, chunk) for n in range(rows.shape[0] // chunk)]
    copies = [
        pltpu.make_async_copy(array.at[pl.ds(start + n * chunk, chunk), :], rows.at[part, :], sems.at[n])
        for n, part in enumerate(parts)
    ]
    for copy in copies:
        copy.start()
    for copy, part in zip(copies, parts):
        copy.wait()
        high[part, :], low[part, :] = split(rows[part, :])


def fetch(array, start, rows, after):
    chunk = LANES
    vmem = pl.BlockSpec(memory_space=pltpu.VMEM)
    shape = (rows, array.shape[1])
    return pl.pallas_call(
        functools.partial(fetch_kernel, start, chunk),
        out_shape=(pltpu.VMEM(shape, jnp.bfloat16), pltpu.VMEM(shape, jnp.bfloat16)),
        in_specs=[pl.BlockSpec(memory_space=pltpu.HBM), vmem],
        out_specs=(vmem, vmem),
        scratch_shapes=[
            pltpu.VMEM(shape, array.dtype),
            pltpu.SemaphoreType.DMA((rows // chunk,)),
        ],
        compiler_params=pltpu.CompilerParams(vmem_limit_bytes=VMEM_LIMIT),
    )(*kept(pltpu.HBM, array), *kept(pltpu.VMEM, after))


def project_kernel(cuts, ids_hbm, act_hbm, pin_hbm, grad_hbm, pout_hbm, out, mask, numbers, ids, act, pin, grad, pout, sems):
    copies = []

    def copy(source, target):
        copies.append(pltpu.make_async_copy(source, target, sems.at[len(copies)]))
        copies[-1].start()
        return copies[-1]

    tokens = copy(ids_hbm, ids)
    left = (copy(pin_hbm, pin), copy(act_hbm, act))
    parts = [pl.ds(start, stop - start) for start, stop in zip(cuts, cuts[1:])]
    right = [
        (copy(pout_hbm.at[:, part], pout.at[:, part]), copy(grad_hbm.at[:, part], grad.at[:, part]))
        for part in parts
    ]
    tokens.wait()
    rows = lax.broadcasted_iota(jnp.int32, mask.shape, 0)
    first = jnp.broadcast_to(ids[:, :1], mask.shape)
    mask[...] = (jnp.broadcast_to(ids[...], mask.shape) - first == rows).astype(jnp.float32)
    shape = numbers.shape
    row = lax.broadcasted_iota(jnp.int32, shape, 0)
    place = row % 2 * LANES + lax.broadcasted_iota(jnp.int32, shape, 1) - SLOTS * position()
    first = jnp.broadcast_to(ids[:, :1], shape)
    value = jnp.where(row < 4, first + place, 1)
    owned = (place >= 0) & (place < SLOTS) & (row % 4 < 2)
    numbers[...] = jnp.where(owned, value, 0).astype(jnp.float32)
    rank = pin.shape[0]
    dims = (((1,), (1,)), ((), ()))
    for piece in left:
        piece.wait()
    out[:rank, :] = lax.dot_general(pin[...], act[...], dims, preferred_element_type=jnp.float32)
    total = None
    for part, pair in zip(parts, right):
        for piece in pair:
            piece.wait()
        term = lax.dot_general(pout[:, part], grad[:, part], dims, preferred_element_type=jnp.float32)
        total = term if total is None else total + term
    out[rank:, :] = total


def project(activations, gradients, proj_in, proj_out, doc_ids):
    tokens, depth = gradients.shape
    rank = proj_in.shape[1]
    cuts = sorted({depth * n // 14 // LANES * LANES for n in (0, 5, 9, 12, 13)} | {depth})
    hbm = pl.BlockSpec(memory_space=pltpu.HBM)
    vmem = pl.BlockSpec(memory_space=pltpu.VMEM)
    return pl.pallas_call(
        functools.partial(project_kernel, cuts),
        out_shape=(
            pltpu.VMEM((2 * rank, tokens), jnp.float32),
            pltpu.VMEM((8, tokens), jnp.float32),
            pltpu.VMEM((8, LANES), jnp.float32),
        ),
        in_specs=[hbm] * 5,
        out_specs=(vmem, vmem, vmem),
        scratch_shapes=[
            pltpu.VMEM((1, tokens), jnp.int32),
            pltpu.VMEM(activations.shape, jnp.bfloat16),
            pltpu.VMEM(proj_in.shape[::-1], jnp.bfloat16),
            pltpu.VMEM(gradients.shape, jnp.bfloat16),
            pltpu.VMEM(proj_out.shape[::-1], jnp.bfloat16),
            pltpu.SemaphoreType.DMA((1 + 2 * len(cuts),)),
        ],
        compiler_params=pltpu.CompilerParams(vmem_limit_bytes=VMEM_LIMIT),
    )(*kept(pltpu.HBM, doc_ids.reshape(1, tokens), activations, proj_in.T, gradients, proj_out.T))


def outer_kernel(part, other, mask, numbers, sums, tags, left):
    rank, tokens = left.shape
    left[...] = part[:rank, :] + other[:rank, :]
    right = part[rank:, :] + other[rank:, :]
    columns = [left[pl.ds(k, rank // 2, stride=2), :] for k in range(2)]
    weighted = jnp.concatenate(
        [jnp.concatenate([half * mask[s : s + 1, :] for half in columns], 1) for s in range(SLOTS)]
    )
    none = jnp.zeros_like(right)
    paired = jnp.concatenate(
        [jnp.concatenate([right, none], 1), jnp.concatenate([none, right], 1)]
    )
    dims = (((1,), (1,)), ((), ()))
    high, low = split(weighted)
    right_high, right_low = split(paired)
    rows = weighted.shape[0]
    found = lax.dot_general(
        jnp.concatenate([high, low]), right_high, dims, preferred_element_type=jnp.float32
    )
    small = lax.dot_general(high, right_low, dims, preferred_element_type=jnp.float32)
    found = found[:rows] + (found[rows:] + small)
    largest = jnp.max(jnp.max(jnp.abs(found), 0, keepdims=True), 1, keepdims=True)
    power = jnp.floor(jnp.log2(jnp.maximum(largest, 1e-30)))
    sums[...] = found * jnp.exp2(TOP - power)
    rows = lax.broadcasted_iota(jnp.int32, numbers.shape, 0)
    tags[...] = numbers[...] * jnp.where(rows < 4, 1.0, jnp.broadcast_to(power, rows.shape))


def outer(part, other, mask, numbers):
    rank, tokens = part.shape[0] // 2, part.shape[1]
    vmem = pl.BlockSpec(memory_space=pltpu.VMEM)
    return pl.pallas_call(
        outer_kernel,
        out_shape=(
            pltpu.VMEM((SLOTS * rank // 2, 2 * rank), jnp.float32),
            pltpu.VMEM(numbers.shape, jnp.float32),
        ),
        in_specs=[vmem] * 4,
        out_specs=(vmem, vmem),
        scratch_shapes=[pltpu.VMEM((rank, tokens), jnp.float32)],
        compiler_params=pltpu.CompilerParams(vmem_limit_bytes=VMEM_LIMIT),
    )(*kept(pltpu.VMEM, part, other, mask, numbers))


def precondition_kernel(windows, own, other, *refs):
    highs, lows, (out, pieces) = refs[:windows], refs[windows : 2 * windows], refs[2 * windows :]
    rows, depth = pieces.shape
    size = own.shape[0] - 8
    count = size * LANES // depth
    pieces[...] = jnp.zeros_like(pieces)
    for k in range(depth // LANES):
        for n, part in enumerate((own, other)):
            pieces[pl.ds(n * count, count), pl.ds(k * LANES, LANES)] = part[
                pl.ds(k, count, stride=depth // LANES), :
            ]
    first, second, at = None, None, 0
    for weights_high, weights_low in zip(highs, lows):
        block = pieces[:, pl.ds(at, weights_high.shape[0])]
        high = block.astype(jnp.bfloat16).astype(jnp.float32)
        both = jnp.concatenate([high, block - high]).astype(jnp.bfloat16)
        term = jnp.dot(both, weights_high[...], preferred_element_type=jnp.float32)
        first = term if first is None else first + term
        upper = both[: pl.cdiv(rows, 16) * 16]
        term = jnp.dot(upper, weights_low[...], preferred_element_type=jnp.float32)
        second = term if second is None else second + term
        at += weights_high.shape[0]
    total = first[:rows] + (first[rows:] + second[:rows])
    marks = []
    for at in (0, 4):
        lanes = [
            jnp.concatenate(
                [part[size + r : size + r + 1, :] for r in range(k, k + pl.cdiv(count // 2, LANES))], 1
            )[:, : count // 2]
            for part in (own, other)
            for k in (at, at + 2)
        ]
        if rows > 2 * count:
            lanes.append(jnp.full((1, rows - 2 * count), -1.0, jnp.float32))
        marks.append(jnp.broadcast_to(jnp.concatenate(lanes, 1), (out.shape[0], rows)))
    numbers, powers = marks
    docs = lax.broadcasted_iota(jnp.int32, numbers.shape, 0).astype(jnp.float32)
    pick = jnp.where(numbers == docs, jnp.exp2(powers - TOP), 0.0).astype(jnp.bfloat16)
    out[...] = sum(jnp.dot(pick, part, preferred_element_type=jnp.float32) for part in split(total))


def precondition(own, other, highs, lows, doc_count):
    vmem = pl.BlockSpec(memory_space=pltpu.VMEM)
    depth, width = sum(high.shape[0] for high in highs), highs[0].shape[1]
    count = (own.shape[0] - 8) * LANES // depth
    return pl.pallas_call(
        functools.partial(precondition_kernel, len(highs)),
        out_shape=pltpu.VMEM((doc_count, width), jnp.float32),
        in_specs=[vmem] * (2 + 2 * len(highs)),
        out_specs=vmem,
        scratch_shapes=[pltpu.VMEM((pl.cdiv(2 * count, 8) * 8, depth), jnp.float32)],
        compiler_params=pltpu.CompilerParams(vmem_limit_bytes=VMEM_LIMIT),
    )(*kept(pltpu.VMEM, own, other, *highs, *lows))


def load_kernel(source, after, target, sem):
    copy = pltpu.make_async_copy(source, target, sem)
    copy.start()
    copy.wait()


def load(array, after):
    vmem = pl.BlockSpec(memory_space=pltpu.VMEM)
    return pl.pallas_call(
        load_kernel,
        out_shape=pltpu.VMEM(array.shape, array.dtype),
        in_specs=[pl.BlockSpec(memory_space=pltpu.HBM), vmem],
        out_specs=vmem,
        scratch_shapes=[pltpu.SemaphoreType.DMA],
        compiler_params=pltpu.CompilerParams(vmem_limit_bytes=VMEM_LIMIT),
    )(*kept(pltpu.HBM, array), *kept(pltpu.VMEM, after))


def column_products(width, rows, held, pair, offsets, store):
    pieces = width // LANES
    bits = held.bit_length() - 1
    total = None
    for n, offset in enumerate(offsets):
        low = (lax.axis_index("ctx") & 3) ^ offset
        blocks, columns = [], [[] for _ in range(pieces)]
        for place in range(held):
            high = sum(((place >> k) & 1) << (bits - 1 - k) for k in range(bits))
            blocks.append(pair[pl.ds((n * held + place) * rows, rows), :])
            for k in range(pieces):
                at = pl.multiple_of((high * 4 + low) * width + k * LANES, LANES)
                columns[k].append(store[:, pl.ds(at, LANES)])
        left = jnp.concatenate(blocks, 1)
        right = jnp.concatenate([jnp.concatenate(column, 1) for column in columns])
        term = lax.dot_general(
            left, right, (((1,), (1,)), ((), ())), preferred_element_type=jnp.float32
        )
        total = term if total is None else total + term
    return total


def held_kernel(width, mine, store, out):
    rows = out.shape[0]
    first = near_distance(lax.axis_index("ctx"), lax.axis_index("col"), 0)
    held = mine.shape[0] // (2 * rows)
    out[...] = column_products(width, rows, held, mine, (0, first), store)


def score_kernel(width, known, theirs, store, out, products):
    rows, count = known.shape[0], store.shape[0]
    pieces = width // LANES
    second = near_distance(lax.axis_index("ctx"), lax.axis_index("col"), 1)
    held = theirs.shape[0] // (2 * rows)
    total = known[...] + column_products(width, rows, held, theirs, (second, 3), store)
    for n in range(products.shape[0] // rows):
        products[pl.ds(n * rows, rows), :] = total[:, n * LANES : (n + 1) * LANES]
    result = None
    for k in range(pieces):
        slab, lane = divmod(k * count, LANES)
        lines = products[pl.ds(slab * rows + k, rows // pieces, stride=pieces), :]
        term = lines[:, lane : lane + count]
        result = term if result is None else result + term
    out[...] = result


def score_held(mine, store, width, doc_count):
    vmem = pl.BlockSpec(memory_space=pltpu.VMEM)
    pieces = width // LANES
    return pl.pallas_call(
        functools.partial(held_kernel, width),
        out_shape=pltpu.VMEM((doc_count * pieces, pieces * store.shape[0]), jnp.float32),
        in_specs=[vmem] * 2,
        out_specs=vmem,
        compiler_params=pltpu.CompilerParams(vmem_limit_bytes=VMEM_LIMIT),
    )(*kept(pltpu.VMEM, mine, store))


def score(known, theirs, store, width, doc_count):
    vmem = pl.BlockSpec(memory_space=pltpu.VMEM)
    slabs = width // LANES * store.shape[0] // LANES
    return pl.pallas_call(
        functools.partial(score_kernel, width),
        out_shape=jax.ShapeDtypeStruct((doc_count, store.shape[0]), jnp.float32),
        in_specs=[vmem] * 3,
        out_specs=vmem,
        scratch_shapes=[pltpu.VMEM((slabs * known.shape[0], LANES), jnp.float32)],
        compiler_params=pltpu.CompilerParams(vmem_limit_bytes=VMEM_LIMIT),
    )(*kept(pltpu.VMEM, known, theirs, store))


def shards(activations, gradients, doc_ids, proj_in, proj_out, inverse, store_rows):
    ctx = lax.axis_size("ctx")
    rank = proj_in.shape[1]
    half = rank // lax.axis_size("col")
    doc_count = SLOTS * ctx // 2
    part, mask, numbers = project(activations, gradients, proj_in, proj_out, doc_ids)
    sums, tags = outer(part, swap_cores(part), mask, numbers)
    blocks, tags = sums.astype(jnp.float16), tags.astype(jnp.float16)
    depth = inverse.shape[0]
    cuts = [0] + [depth * k // 8 // LANES * LANES for k in ((2, 5) if far_distances() else (4,))] + [depth]
    highs, lows = [], []

    def beside(exchange, payload, ready):
        other, at = exchange(payload), len(highs)
        pair = fetch(inverse, cuts[at], cuts[at + 1] - cuts[at], ready)
        other, high, low = lax.optimization_barrier((other, *pair))
        highs.append(high)
        lows.append(low)
        return other

    for distance in far_distances():
        size = blocks.shape[0]
        exchange = functools.partial(swap_far, distance=distance)
        payload = jnp.concatenate([blocks, tags])
        if distance == far_distances()[-1]:
            other = beside(exchange, payload, tags.astype(jnp.float32))
        else:
            other = exchange(payload)
        blocks = ordered(blocks, other[:size], distance)
        tags = tags + other[size:]
    size = blocks.shape[0]
    payload = jnp.concatenate([blocks, tags])
    other = beside(functools.partial(swap_near, last=0), payload, tags.astype(jnp.float32))
    blocks = jnp.concatenate([blocks, other[:size]])
    tags = tags + jnp.roll(other[size:], 2, 0)
    halves = blocks.reshape(-1, 2, half * rank // LANES, LANES)
    first = lax.axis_index("col") == 0
    own = jnp.where(first, halves[:, 0], halves[:, 1]).reshape(-1, LANES)
    others = jnp.where(first, halves[:, 1], halves[:, 0]).reshape(-1, LANES)
    own = jnp.concatenate([own, tags]).astype(jnp.float32)
    other = beside(functools.partial(swap_near, last=1), jnp.concatenate([others, tags]), own)
    partial_q = precondition(own, other.astype(jnp.float32), highs, lows, doc_count)
    precond = (partial_q + swap_cores(partial_q)).astype(jnp.bfloat16)
    width = precond.shape[1]
    whole = precond.reshape(-1, min(width, LANES))
    count = store_rows.shape[0]
    direct = width % LANES == 0 and LANES % count == 0 and width * count % LANES**2 == 0
    if direct:
        store = load(store_rows, whole)
    for step, distance in enumerate(far_distances()):
        other = swap_far(whole, distance)
        if direct and step == 0:
            other, store = lax.optimization_barrier((other, store))
        whole = ordered(whole, other, distance)
    whole = jnp.concatenate([whole, swap_near(whole, 0)])
    others = swap_near(whole, 1)
    if direct:
        known = score_held(whole, store, width, doc_count)
        others, known = lax.optimization_barrier((others, known))
        return score(known, others, store, width, doc_count)
    (own, near), (next_one, farthest) = (x.reshape(2, -1, x.shape[1]) for x in (whole, others))
    c, p = lax.axis_index("ctx"), lax.axis_index("col")
    single = near_distance(c, p, 0) == 1
    near, next_one = jnp.where(single, near, next_one), jnp.where(single, next_one, near)
    whole = jnp.stack([own, near, next_one, farthest])
    for bit in (1, 2):
        pairs = whole.reshape((2 // bit, 2, bit) + whole.shape[1:])
        whole = jnp.where((c & bit) != 0, pairs[:, ::-1], pairs).reshape(whole.shape)
    bits = len(far_distances())
    whole = whole.reshape((4,) + (2,) * bits + (doc_count, width))
    whole = whole.transpose((bits + 1,) + tuple(range(1, bits + 1))[::-1] + (0, bits + 2))
    whole = whole.reshape(doc_count, -1)
    return lax.dot_general(
        whole, store_rows, (((1,), (1,)), ((), ())), preferred_element_type=jnp.float32
    )


def solution(mesh):
    in_specs = (
        P(("groups", "ctx"), "col"),
        P(("groups", "ctx"), "col"),
        P(("groups", "ctx")),
        P("col", None),
        P("col", None),
        P("col", "ctx"),
        P(("groups", "ctx", "col"), None),
    )
    out_specs = P(None, ("groups", "ctx", "col"))
    return jax.shard_map(shards, mesh=mesh, in_specs=in_specs, out_specs=out_specs, check_vma=False)
```

```python
import functools

import jax
import jax.numpy as jnp
from jax import lax
from jax.experimental import pallas as pl
from jax.experimental.pallas import tpu as pltpu
from jax.sharding import PartitionSpec as P

SLOTS = 3
LANES = 128
TOP = 13.0
VMEM_LIMIT = 16 << 20


def plans():
    size = lax.axis_size("ctx")
    far = [size >> step for step in range(1, size.bit_length() - 3)]
    return far + [4, 1, 2], far + [2, 4, 1]


def family(c, p):
    total = p
    for step in range(lax.axis_size("ctx").bit_length() - 1):
        total = total ^ (c >> step)
    return total & 1


def swap(block, partner):
    ctx, col = lax.axis_size("ctx"), lax.axis_size("col")
    route = []
    for c in range(ctx):
        for p in range(col):
            there, core = partner(c, p)
            route.append((c * col + p, there * col + core))
    return lax.ppermute(block, ("ctx", "col"), route)


def swap_cores(block):
    return swap(block, lambda c, p: (c, p ^ 1))


def exchange(block, turn):
    both = plans()
    return swap(block, lambda c, p: (c ^ both[family(c, p)][turn], p ^ 1))


def owner(place):
    c = lax.axis_index("ctx")
    second = family(c, lax.axis_index("col"))
    for turn, (one, two) in enumerate(zip(*plans())):
        if (place >> turn) & 1:
            c = c ^ (one + (two - one) * second)
    return c


def kept(space, *arrays):
    return [pltpu.with_memory_space_constraint(array, space) for array in arrays]


def split(array):
    high = array.astype(jnp.bfloat16)
    return high, (array - high.astype(jnp.float32)).astype(jnp.bfloat16)


def fetch_kernel(start, chunk, array, after, high, low, rows, sems):
    parts = [pl.ds(n * chunk, chunk) for n in range(rows.shape[0] // chunk)]
    copies = [
        pltpu.make_async_copy(array.at[pl.ds(start + n * chunk, chunk), :], rows.at[part, :], sems.at[n])
        for n, part in enumerate(parts)
    ]
    for copy in copies:
        copy.start()
    for copy, part in zip(copies, parts):
        copy.wait()
        high[part, :], low[part, :] = split(rows[part, :])


def fetch(array, start, rows, after):
    chunk = LANES
    vmem = pl.BlockSpec(memory_space=pltpu.VMEM)
    shape = (rows, array.shape[1])
    return pl.pallas_call(
        functools.partial(fetch_kernel, start, chunk),
        out_shape=(pltpu.VMEM(shape, jnp.bfloat16), pltpu.VMEM(shape, jnp.bfloat16)),
        in_specs=[pl.BlockSpec(memory_space=pltpu.HBM), vmem],
        out_specs=(vmem, vmem),
        scratch_shapes=[
            pltpu.VMEM(shape, array.dtype),
            pltpu.SemaphoreType.DMA((rows // chunk,)),
        ],
        compiler_params=pltpu.CompilerParams(vmem_limit_bytes=VMEM_LIMIT),
    )(*kept(pltpu.HBM, array), *kept(pltpu.VMEM, after))


def project_kernel(cuts, ids_hbm, act_hbm, pin_hbm, grad_hbm, pout_hbm, out, mask, numbers, ids, act, pin, grad, pout, sems):
    copies = []

    def copy(source, target):
        copies.append(pltpu.make_async_copy(source, target, sems.at[len(copies)]))
        copies[-1].start()
        return copies[-1]

    tokens = copy(ids_hbm, ids)
    left = (copy(pin_hbm, pin), copy(act_hbm, act))
    parts = [pl.ds(start, stop - start) for start, stop in zip(cuts, cuts[1:])]
    right = [
        (copy(pout_hbm.at[:, part], pout.at[:, part]), copy(grad_hbm.at[:, part], grad.at[:, part]))
        for part in parts
    ]
    tokens.wait()
    rows = lax.broadcasted_iota(jnp.int32, mask.shape, 0)
    first = jnp.broadcast_to(ids[:, :1], mask.shape)
    mask[...] = (jnp.broadcast_to(ids[...], mask.shape) - first == rows).astype(jnp.float32)
    shape = numbers.shape
    row = lax.broadcasted_iota(jnp.int32, shape, 0)
    place = row % 2 * LANES + lax.broadcasted_iota(jnp.int32, shape, 1)
    first = jnp.broadcast_to(ids[:, :1], shape)
    value = jnp.where(row < 4, first + place, 1)
    owned = (place >= 0) & (place < SLOTS) & (row % 4 < 2)
    numbers[...] = jnp.where(owned, value, 0).astype(jnp.float32)
    rank = pin.shape[0]
    dims = (((1,), (1,)), ((), ()))
    for piece in left:
        piece.wait()
    out[:rank, :] = lax.dot_general(pin[...], act[...], dims, preferred_element_type=jnp.float32)
    total = None
    for part, pair in zip(parts, right):
        for piece in pair:
            piece.wait()
        term = lax.dot_general(pout[:, part], grad[:, part], dims, preferred_element_type=jnp.float32)
        total = term if total is None else total + term
    out[rank:, :] = total


def project(activations, gradients, proj_in, proj_out, doc_ids):
    tokens, depth = gradients.shape
    rank = proj_in.shape[1]
    cuts = sorted({depth * n // 14 // LANES * LANES for n in (0, 5, 9, 12, 13)} | {depth})
    hbm = pl.BlockSpec(memory_space=pltpu.HBM)
    vmem = pl.BlockSpec(memory_space=pltpu.VMEM)
    return pl.pallas_call(
        functools.partial(project_kernel, cuts),
        out_shape=(
            pltpu.VMEM((2 * rank, tokens), jnp.float32),
            pltpu.VMEM((8, tokens), jnp.float32),
            pltpu.VMEM((8, LANES), jnp.float32),
        ),
        in_specs=[hbm] * 5,
        out_specs=(vmem, vmem, vmem),
        scratch_shapes=[
            pltpu.VMEM((1, tokens), jnp.int32),
            pltpu.VMEM(activations.shape, jnp.bfloat16),
            pltpu.VMEM(proj_in.shape[::-1], jnp.bfloat16),
            pltpu.VMEM(gradients.shape, jnp.bfloat16),
            pltpu.VMEM(proj_out.shape[::-1], jnp.bfloat16),
            pltpu.SemaphoreType.DMA((1 + 2 * len(cuts),)),
        ],
        compiler_params=pltpu.CompilerParams(vmem_limit_bytes=VMEM_LIMIT),
    )(*kept(pltpu.HBM, doc_ids.reshape(1, tokens), activations, proj_in.T, gradients, proj_out.T))


def outer_kernel(part, other, mask, numbers, sums, tags, left):
    rank, tokens = left.shape
    left[...] = part[:rank, :] + other[:rank, :]
    right = part[rank:, :] + other[rank:, :]
    columns = [left[pl.ds(k, rank // 2, stride=2), :] for k in range(2)]
    weighted = jnp.concatenate(
        [jnp.concatenate([half * mask[s : s + 1, :] for half in columns], 1) for s in range(SLOTS)]
    )
    none = jnp.zeros_like(right)
    paired = jnp.concatenate(
        [jnp.concatenate([right, none], 1), jnp.concatenate([none, right], 1)]
    )
    dims = (((1,), (1,)), ((), ()))
    high, low = split(weighted)
    right_high, right_low = split(paired)
    rows = weighted.shape[0]
    found = lax.dot_general(
        jnp.concatenate([high, low]), right_high, dims, preferred_element_type=jnp.float32
    )
    small = lax.dot_general(high, right_low, dims, preferred_element_type=jnp.float32)
    found = found[:rows] + (found[rows:] + small)
    largest = jnp.max(jnp.max(jnp.abs(found), 0, keepdims=True), 1, keepdims=True)
    power = jnp.floor(jnp.log2(jnp.maximum(largest, 1e-30)))
    sums[...] = found * jnp.exp2(TOP - power)
    rows = lax.broadcasted_iota(jnp.int32, numbers.shape, 0)
    tags[...] = numbers[...] * jnp.where(rows < 4, 1.0, jnp.broadcast_to(power, rows.shape))


def outer(part, other, mask, numbers):
    rank, tokens = part.shape[0] // 2, part.shape[1]
    vmem = pl.BlockSpec(memory_space=pltpu.VMEM)
    return pl.pallas_call(
        outer_kernel,
        out_shape=(
            pltpu.VMEM((SLOTS * rank // 2, 2 * rank), jnp.float32),
            pltpu.VMEM(numbers.shape, jnp.float32),
        ),
        in_specs=[vmem] * 4,
        out_specs=(vmem, vmem),
        scratch_shapes=[pltpu.VMEM((rank, tokens), jnp.float32)],
        compiler_params=pltpu.CompilerParams(vmem_limit_bytes=VMEM_LIMIT),
    )(*kept(pltpu.VMEM, part, other, mask, numbers))


def precondition_kernel(windows, own, other, *refs):
    highs, lows, (out, pieces) = refs[:windows], refs[windows : 2 * windows], refs[2 * windows :]
    rows, depth = pieces.shape
    size = own.shape[0] - 8
    count = size * LANES // depth
    pieces[...] = jnp.zeros_like(pieces)
    for k in range(depth // LANES):
        for n, part in enumerate((own, other)):
            pieces[pl.ds(n * count, count), pl.ds(k * LANES, LANES)] = part[
                pl.ds(k, count, stride=depth // LANES), :
            ]
    first, second, at = None, None, 0
    for weights_high, weights_low in zip(highs, lows):
        block = pieces[:, pl.ds(at, weights_high.shape[0])]
        high = block.astype(jnp.bfloat16).astype(jnp.float32)
        both = jnp.concatenate([high, block - high]).astype(jnp.bfloat16)
        term = jnp.dot(both, weights_high[...], preferred_element_type=jnp.float32)
        first = term if first is None else first + term
        upper = both[: pl.cdiv(rows, 16) * 16]
        term = jnp.dot(upper, weights_low[...], preferred_element_type=jnp.float32)
        second = term if second is None else second + term
        at += weights_high.shape[0]
    total = first[:rows] + (first[rows:] + second[:rows])
    marks = []
    for at in (0, 4):
        lanes = [
            jnp.concatenate(
                [part[size + r : size + r + 1, :] for r in range(k, k + pl.cdiv(count // 2, LANES))], 1
            )[:, : count // 2]
            for part in (own, other)
            for k in (at, at + 2)
        ]
        if rows > 2 * count:
            lanes.append(jnp.full((1, rows - 2 * count), -1.0, jnp.float32))
        marks.append(jnp.broadcast_to(jnp.concatenate(lanes, 1), (out.shape[0], rows)))
    numbers, powers = marks
    docs = lax.broadcasted_iota(jnp.int32, numbers.shape, 0).astype(jnp.float32)
    pick = jnp.where(numbers == docs, jnp.exp2(powers - TOP), 0.0).astype(jnp.bfloat16)
    out[...] = sum(jnp.dot(pick, part, preferred_element_type=jnp.float32) for part in split(total))


def precondition(own, other, highs, lows, doc_count):
    vmem = pl.BlockSpec(memory_space=pltpu.VMEM)
    depth, width = sum(high.shape[0] for high in highs), highs[0].shape[1]
    count = (own.shape[0] - 8) * LANES // depth
    return pl.pallas_call(
        functools.partial(precondition_kernel, len(highs)),
        out_shape=pltpu.VMEM((doc_count, width), jnp.float32),
        in_specs=[vmem] * (2 + 2 * len(highs)),
        out_specs=vmem,
        scratch_shapes=[pltpu.VMEM((pl.cdiv(2 * count, 8) * 8, depth), jnp.float32)],
        compiler_params=pltpu.CompilerParams(vmem_limit_bytes=VMEM_LIMIT),
    )(*kept(pltpu.VMEM, own, other, *highs, *lows))


def load_kernel(source, after, target, sem):
    copy = pltpu.make_async_copy(source, target, sem)
    copy.start()
    copy.wait()


def load(array, after):
    vmem = pl.BlockSpec(memory_space=pltpu.VMEM)
    return pl.pallas_call(
        load_kernel,
        out_shape=pltpu.VMEM(array.shape, array.dtype),
        in_specs=[pl.BlockSpec(memory_space=pltpu.HBM), vmem],
        out_specs=vmem,
        scratch_shapes=[pltpu.SemaphoreType.DMA],
        compiler_params=pltpu.CompilerParams(vmem_limit_bytes=VMEM_LIMIT),
    )(*kept(pltpu.HBM, array), *kept(pltpu.VMEM, after))


def column_products(width, rows, start, blocks, store):
    pieces = width // LANES
    total = None
    for pair in range(0, blocks.shape[0] // rows, 2):
        columns = [[] for _ in range(pieces)]
        for place in (pair, pair + 1):
            shard = owner(start + place)
            for k in range(pieces):
                at = pl.multiple_of(shard * width + k * LANES, LANES)
                columns[k].append(store[:, pl.ds(at, LANES)])
        left = jnp.concatenate([blocks[pl.ds((pair + n) * rows, rows), :] for n in range(2)], 1)
        right = jnp.concatenate([jnp.concatenate(column, 1) for column in columns])
        term = lax.dot_general(
            left, right, (((1,), (1,)), ((), ())), preferred_element_type=jnp.float32
        )
        total = term if total is None else total + term
    return total


def held_kernel(width, mine, store, out):
    out[...] = column_products(width, out.shape[0], 0, mine, store)


def score_kernel(width, known, theirs, store, out, products):
    rows, count = known.shape[0], store.shape[0]
    pieces = width // LANES
    total = known[...] + column_products(width, rows, theirs.shape[0] // rows, theirs, store)
    for n in range(products.shape[0] // rows):
        products[pl.ds(n * rows, rows), :] = total[:, n * LANES : (n + 1) * LANES]
    result = None
    for k in range(pieces):
        slab, lane = divmod(k * count, LANES)
        lines = products[pl.ds(slab * rows + k, rows // pieces, stride=pieces), :]
        term = lines[:, lane : lane + count]
        result = term if result is None else result + term
    out[...] = result


def score_held(mine, store, width, doc_count):
    vmem = pl.BlockSpec(memory_space=pltpu.VMEM)
    pieces = width // LANES
    return pl.pallas_call(
        functools.partial(held_kernel, width),
        out_shape=pltpu.VMEM((doc_count * pieces, pieces * store.shape[0]), jnp.float32),
        in_specs=[vmem] * 2,
        out_specs=vmem,
        compiler_params=pltpu.CompilerParams(vmem_limit_bytes=VMEM_LIMIT),
    )(*kept(pltpu.VMEM, mine, store))


def score(known, theirs, store, width, doc_count):
    vmem = pl.BlockSpec(memory_space=pltpu.VMEM)
    slabs = width // LANES * store.shape[0] // LANES
    return pl.pallas_call(
        functools.partial(score_kernel, width),
        out_shape=jax.ShapeDtypeStruct((doc_count, store.shape[0]), jnp.float32),
        in_specs=[vmem] * 3,
        out_specs=vmem,
        scratch_shapes=[pltpu.VMEM((slabs * known.shape[0], LANES), jnp.float32)],
        compiler_params=pltpu.CompilerParams(vmem_limit_bytes=VMEM_LIMIT),
    )(*kept(pltpu.VMEM, known, theirs, store))


def shards(activations, gradients, doc_ids, proj_in, proj_out, inverse, store_rows):
    ctx = lax.axis_size("ctx")
    rank = proj_in.shape[1]
    half = rank // lax.axis_size("col")
    doc_count = SLOTS * ctx // 2
    part, mask, numbers = project(activations, gradients, proj_in, proj_out, doc_ids)
    sums, tags = outer(part, swap_cores(part), mask, numbers)
    blocks, tags = sums.astype(jnp.float16), tags.astype(jnp.float16)
    depth = inverse.shape[0]
    turns = len(plans()[0])
    cuts = [0] + [depth * k // 8 // LANES * LANES for k in (2, 5)] + [depth]
    highs, lows = [], []

    def beside(payload, turn, ready):
        other, at = exchange(payload, turn), len(highs)
        pair = fetch(inverse, cuts[at], cuts[at + 1] - cuts[at], ready)
        other, high, low = lax.optimization_barrier((other, *pair))
        highs.append(high)
        lows.append(low)
        return other

    for turn in range(turns - 1):
        size = blocks.shape[0]
        payload = jnp.concatenate([blocks, tags])
        if turn < turns - 3:
            other = exchange(payload, turn)
        else:
            other = beside(payload, turn, tags.astype(jnp.float32))
        blocks = jnp.concatenate([blocks, other[:size]])
        if turn < turns - 2:
            tags = tags + jnp.roll(other[size:], SLOTS << turn, 1)
        else:
            tags = tags + jnp.roll(other[size:], 2, 0)
    halves = blocks.reshape(-1, 2, half * rank // LANES, LANES)
    first = lax.axis_index("col") == 0
    own = jnp.where(first, halves[:, 0], halves[:, 1]).reshape(-1, LANES)
    others = jnp.where(first, halves[:, 1], halves[:, 0]).reshape(-1, LANES)
    own = jnp.concatenate([own, tags]).astype(jnp.float32)
    other = beside(jnp.concatenate([others, tags]), turns - 1, own)
    partial_q = precondition(own, other.astype(jnp.float32), highs, lows, doc_count)
    precond = (partial_q + swap_cores(partial_q)).astype(jnp.bfloat16)
    width = precond.shape[1]
    whole = precond.reshape(-1, min(width, LANES))
    count = store_rows.shape[0]
    direct = width % LANES == 0 and LANES % count == 0 and width * count % LANES**2 == 0
    if direct:
        store = load(store_rows, whole)
    for turn in range(turns - 1):
        other = exchange(whole, turn)
        if direct and turn == 0:
            other, store = lax.optimization_barrier((other, store))
        whole = jnp.concatenate([whole, other])
    others = exchange(whole, turns - 1)
    if direct:
        known = score_held(whole, store, width, doc_count)
        others, known = lax.optimization_barrier((others, known))
        return score(known, others, store, width, doc_count)
    whole = jnp.concatenate([whole, others]).reshape(ctx, doc_count, width)
    owners = jnp.stack([owner(place) for place in range(ctx)])
    found = owners[None, :] == jnp.arange(ctx, dtype=owners.dtype)[:, None]
    whole = jnp.take(whole, jnp.argmax(found, axis=1), axis=0)
    whole = whole.transpose(1, 0, 2).reshape(doc_count, -1)
    return lax.dot_general(
        whole, store_rows, (((1,), (1,)), ((), ())), preferred_element_type=jnp.float32
    )


def solution(mesh):
    in_specs = (
        P(("groups", "ctx"), "col"),
        P(("groups", "ctx"), "col"),
        P(("groups", "ctx")),
        P("col", None),
        P("col", None),
        P("col", "ctx"),
        P(("groups", "ctx", "col"), None),
    )
    out_specs = P(None, ("groups", "ctx", "col"))
    return jax.shard_map(shards, mesh=mesh, in_specs=in_specs, out_specs=out_specs, check_vma=False)
```

```python
import functools

import jax
import jax.numpy as jnp
from jax import lax
from jax.experimental import pallas as pl
from jax.experimental.pallas import tpu as pltpu
from jax.sharding import PartitionSpec as P

SLOTS = 3
LANES = 128
TOP = 13.0
VMEM_LIMIT = 16 << 20


def plans():
    size = lax.axis_size("ctx")
    far = [size >> step for step in range(1, size.bit_length() - 3)]
    return far + [4, 1, 2], far + [2, 4, 1]


def family(c, p):
    total = p
    for step in range(lax.axis_size("ctx").bit_length() - 1):
        total = total ^ (c >> step)
    return total & 1


def swap(block, partner):
    ctx, col = lax.axis_size("ctx"), lax.axis_size("col")
    route = []
    for c in range(ctx):
        for p in range(col):
            there, core = partner(c, p)
            route.append((c * col + p, there * col + core))
    return lax.ppermute(block, ("ctx", "col"), route)


def swap_cores(block):
    return swap(block, lambda c, p: (c, p ^ 1))


def exchange(block, turn):
    both = plans()
    return swap(block, lambda c, p: (c ^ both[family(c, p)][turn], p ^ 1))


def owner(place):
    c = lax.axis_index("ctx")
    second = family(c, lax.axis_index("col"))
    for turn, (one, two) in enumerate(zip(*plans())):
        if (place >> turn) & 1:
            c = c ^ (one + (two - one) * second)
    return c


def kept(space, *arrays):
    return [pltpu.with_memory_space_constraint(array, space) for array in arrays]


def split(array):
    high = array.astype(jnp.bfloat16)
    return high, (array - high.astype(jnp.float32)).astype(jnp.bfloat16)


def fetch_kernel(start, chunk, array, after, high, low, rows, sems):
    parts = [pl.ds(n * chunk, chunk) for n in range(rows.shape[0] // chunk)]
    copies = [
        pltpu.make_async_copy(array.at[pl.ds(start + n * chunk, chunk), :], rows.at[part, :], sems.at[n])
        for n, part in enumerate(parts)
    ]
    for copy in copies:
        copy.start()
    for copy, part in zip(copies, parts):
        copy.wait()
        high[part, :], low[part, :] = split(rows[part, :])


def fetch(array, start, rows, after):
    chunk = LANES
    vmem = pl.BlockSpec(memory_space=pltpu.VMEM)
    shape = (rows, array.shape[1])
    return pl.pallas_call(
        functools.partial(fetch_kernel, start, chunk),
        out_shape=(pltpu.VMEM(shape, jnp.bfloat16), pltpu.VMEM(shape, jnp.bfloat16)),
        in_specs=[pl.BlockSpec(memory_space=pltpu.HBM), vmem],
        out_specs=(vmem, vmem),
        scratch_shapes=[
            pltpu.VMEM(shape, array.dtype),
            pltpu.SemaphoreType.DMA((rows // chunk,)),
        ],
        compiler_params=pltpu.CompilerParams(vmem_limit_bytes=VMEM_LIMIT),
    )(*kept(pltpu.HBM, array), *kept(pltpu.VMEM, after))


def project_kernel(cuts, ids_hbm, act_hbm, pin_hbm, grad_hbm, pout_hbm, out, mask, numbers, ids, act, pin, grad, pout, sems):
    copies = []

    def copy(source, target):
        copies.append(pltpu.make_async_copy(source, target, sems.at[len(copies)]))
        copies[-1].start()
        return copies[-1]

    tokens = copy(ids_hbm, ids)
    left = (copy(pin_hbm, pin), copy(act_hbm, act))
    parts = [pl.ds(start, stop - start) for start, stop in zip(cuts, cuts[1:])]
    right = [
        (copy(pout_hbm.at[:, part], pout.at[:, part]), copy(grad_hbm.at[:, part], grad.at[:, part]))
        for part in parts
    ]
    tokens.wait()
    rows = lax.broadcasted_iota(jnp.int32, mask.shape, 0)
    first = jnp.broadcast_to(ids[:, :1], mask.shape)
    mask[...] = (jnp.broadcast_to(ids[...], mask.shape) - first == rows).astype(jnp.float32)
    shape = numbers.shape
    row = lax.broadcasted_iota(jnp.int32, shape, 0)
    place = row % 2 * LANES + lax.broadcasted_iota(jnp.int32, shape, 1)
    first = jnp.broadcast_to(ids[:, :1], shape)
    value = jnp.where(row < 4, first + place, 1)
    owned = (place >= 0) & (place < SLOTS) & (row % 4 < 2)
    numbers[...] = jnp.where(owned, value, 0).astype(jnp.float32)
    rank = pin.shape[0]
    dims = (((1,), (1,)), ((), ()))
    for piece in left:
        piece.wait()
    out[:rank, :] = lax.dot_general(pin[...], act[...], dims, preferred_element_type=jnp.float32)
    total = None
    for part, pair in zip(parts, right):
        for piece in pair:
            piece.wait()
        term = lax.dot_general(pout[:, part], grad[:, part], dims, preferred_element_type=jnp.float32)
        total = term if total is None else total + term
    out[rank:, :] = total


def project(activations, gradients, proj_in, proj_out, doc_ids):
    tokens, depth = gradients.shape
    rank = proj_in.shape[1]
    cuts = sorted({depth * n // 14 // LANES * LANES for n in (0, 5, 9, 12, 13)} | {depth})
    hbm = pl.BlockSpec(memory_space=pltpu.HBM)
    vmem = pl.BlockSpec(memory_space=pltpu.VMEM)
    return pl.pallas_call(
        functools.partial(project_kernel, cuts),
        out_shape=(
            pltpu.VMEM((2 * rank, tokens), jnp.float32),
            pltpu.VMEM((8, tokens), jnp.float32),
            pltpu.VMEM((8, LANES), jnp.float32),
        ),
        in_specs=[hbm] * 5,
        out_specs=(vmem, vmem, vmem),
        scratch_shapes=[
            pltpu.VMEM((1, tokens), jnp.int32),
            pltpu.VMEM(activations.shape, jnp.bfloat16),
            pltpu.VMEM(proj_in.shape[::-1], jnp.bfloat16),
            pltpu.VMEM(gradients.shape, jnp.bfloat16),
            pltpu.VMEM(proj_out.shape[::-1], jnp.bfloat16),
            pltpu.SemaphoreType.DMA((1 + 2 * len(cuts),)),
        ],
        compiler_params=pltpu.CompilerParams(vmem_limit_bytes=VMEM_LIMIT),
    )(*kept(pltpu.HBM, doc_ids.reshape(1, tokens), activations, proj_in.T, gradients, proj_out.T))


def outer_kernel(part, other, mask, numbers, sums, tags, left):
    rank, tokens = left.shape
    left[...] = part[:rank, :] + other[:rank, :]
    right = part[rank:, :] + other[rank:, :]
    columns = [left[pl.ds(k, rank // 2, stride=2), :] for k in range(2)]
    weighted = jnp.concatenate(
        [jnp.concatenate([half * mask[s : s + 1, :] for half in columns], 1) for s in range(SLOTS)]
    )
    none = jnp.zeros_like(right)
    paired = jnp.concatenate(
        [jnp.concatenate([right, none], 1), jnp.concatenate([none, right], 1)]
    )
    dims = (((1,), (1,)), ((), ()))
    high, low = split(weighted)
    right_high, right_low = split(paired)
    rows = weighted.shape[0]
    found = lax.dot_general(
        jnp.concatenate([high, low]), right_high, dims, preferred_element_type=jnp.float32
    )
    small = lax.dot_general(high, right_low, dims, preferred_element_type=jnp.float32)
    found = found[:rows] + (found[rows:] + small)
    largest = jnp.max(jnp.max(jnp.abs(found), 0, keepdims=True), 1, keepdims=True)
    power = jnp.floor(jnp.log2(jnp.maximum(largest, 1e-30)))
    sums[...] = found * jnp.exp2(TOP - power)
    rows = lax.broadcasted_iota(jnp.int32, numbers.shape, 0)
    tags[...] = numbers[...] * jnp.where(rows < 4, 1.0, jnp.broadcast_to(power, rows.shape))


def outer(part, other, mask, numbers):
    rank, tokens = part.shape[0] // 2, part.shape[1]
    vmem = pl.BlockSpec(memory_space=pltpu.VMEM)
    return pl.pallas_call(
        outer_kernel,
        out_shape=(
            pltpu.VMEM((SLOTS * rank // 2, 2 * rank), jnp.float32),
            pltpu.VMEM(numbers.shape, jnp.float32),
        ),
        in_specs=[vmem] * 4,
        out_specs=(vmem, vmem),
        scratch_shapes=[pltpu.VMEM((rank, tokens), jnp.float32)],
        compiler_params=pltpu.CompilerParams(vmem_limit_bytes=VMEM_LIMIT),
    )(*kept(pltpu.VMEM, part, other, mask, numbers))


def precondition_kernel(windows, own, other, *refs):
    highs, lows, (out, pieces) = refs[:windows], refs[windows : 2 * windows], refs[2 * windows :]
    rows, depth = pieces.shape
    size = own.shape[0] - 8
    count = size * LANES // depth
    if rows > 2 * count:
        pieces[...] = jnp.zeros_like(pieces)
    for k in range(depth // LANES):
        for n, part in enumerate((own, other)):
            pieces[pl.ds(n * count, count), pl.ds(k * LANES, LANES)] = part[
                pl.ds(k, count, stride=depth // LANES), :
            ]
    first, second, at = None, None, 0
    for weights_high, weights_low in zip(highs, lows):
        block = pieces[:, pl.ds(at, weights_high.shape[0])]
        high = block.astype(jnp.bfloat16).astype(jnp.float32)
        both = jnp.concatenate([high, block - high]).astype(jnp.bfloat16)
        term = jnp.dot(both, weights_high[...], preferred_element_type=jnp.float32)
        first = term if first is None else first + term
        upper = both[: pl.cdiv(rows, 16) * 16]
        term = jnp.dot(upper, weights_low[...], preferred_element_type=jnp.float32)
        second = term if second is None else second + term
        at += weights_high.shape[0]
    total = first[:rows] + (first[rows:] + second[:rows])
    marks = []
    for at in (0, 4):
        lanes = [
            jnp.concatenate(
                [part[size + r : size + r + 1, :] for r in range(k, k + pl.cdiv(count // 2, LANES))], 1
            )[:, : count // 2]
            for part in (own, other)
            for k in (at, at + 2)
        ]
        if rows > 2 * count:
            lanes.append(jnp.full((1, rows - 2 * count), -1.0, jnp.float32))
        marks.append(jnp.broadcast_to(jnp.concatenate(lanes, 1), (out.shape[0], rows)))
    numbers, powers = marks
    docs = lax.broadcasted_iota(jnp.int32, numbers.shape, 0).astype(jnp.float32)
    pick = jnp.where(numbers == docs, jnp.exp2(powers - TOP), 0.0).astype(jnp.bfloat16)
    out[...] = sum(jnp.dot(pick, part, preferred_element_type=jnp.float32) for part in split(total))


def precondition(own, other, highs, lows, doc_count):
    vmem = pl.BlockSpec(memory_space=pltpu.VMEM)
    depth, width = sum(high.shape[0] for high in highs), highs[0].shape[1]
    count = (own.shape[0] - 8) * LANES // depth
    return pl.pallas_call(
        functools.partial(precondition_kernel, len(highs)),
        out_shape=pltpu.VMEM((doc_count, width), jnp.float32),
        in_specs=[vmem] * (2 + 2 * len(highs)),
        out_specs=vmem,
        scratch_shapes=[pltpu.VMEM((pl.cdiv(2 * count, 8) * 8, depth), jnp.float32)],
        compiler_params=pltpu.CompilerParams(vmem_limit_bytes=VMEM_LIMIT),
    )(*kept(pltpu.VMEM, own, other, *highs, *lows))


def load_kernel(source, after, target, sem):
    copy = pltpu.make_async_copy(source, target, sem)
    copy.start()
    copy.wait()


def load(array, after):
    vmem = pl.BlockSpec(memory_space=pltpu.VMEM)
    return pl.pallas_call(
        load_kernel,
        out_shape=pltpu.VMEM(array.shape, array.dtype),
        in_specs=[pl.BlockSpec(memory_space=pltpu.HBM), vmem],
        out_specs=vmem,
        scratch_shapes=[pltpu.SemaphoreType.DMA],
        compiler_params=pltpu.CompilerParams(vmem_limit_bytes=VMEM_LIMIT),
    )(*kept(pltpu.HBM, array), *kept(pltpu.VMEM, after))


def column_products(width, rows, start, blocks, store):
    pieces = width // LANES
    total = None
    for pair in range(0, blocks.shape[0] // rows, 2):
        columns = [[] for _ in range(pieces)]
        for place in (pair, pair + 1):
            shard = owner(start + place)
            for k in range(pieces):
                at = pl.multiple_of(shard * width + k * LANES, LANES)
                columns[k].append(store[:, pl.ds(at, LANES)])
        left = jnp.concatenate([blocks[pl.ds((pair + n) * rows, rows), :] for n in range(2)], 1)
        right = jnp.concatenate([jnp.concatenate(column, 1) for column in columns])
        term = lax.dot_general(
            left, right, (((1,), (1,)), ((), ())), preferred_element_type=jnp.float32
        )
        total = term if total is None else total + term
    return total


def held_kernel(width, mine, store, out):
    out[...] = column_products(width, out.shape[0], 0, mine, store)


def score_kernel(width, known, theirs, store, out, products):
    rows, count = known.shape[0], store.shape[0]
    pieces = width // LANES
    total = known[...] + column_products(width, rows, theirs.shape[0] // rows, theirs, store)
    for n in range(products.shape[0] // rows):
        products[pl.ds(n * rows, rows), :] = total[:, n * LANES : (n + 1) * LANES]
    result = None
    for k in range(pieces):
        slab, lane = divmod(k * count, LANES)
        lines = products[pl.ds(slab * rows + k, rows // pieces, stride=pieces), :]
        term = lines[:, lane : lane + count]
        result = term if result is None else result + term
    out[...] = result


def score_held(mine, store, width, doc_count):
    vmem = pl.BlockSpec(memory_space=pltpu.VMEM)
    pieces = width // LANES
    return pl.pallas_call(
        functools.partial(held_kernel, width),
        out_shape=pltpu.VMEM((doc_count * pieces, pieces * store.shape[0]), jnp.float32),
        in_specs=[vmem] * 2,
        out_specs=vmem,
        compiler_params=pltpu.CompilerParams(vmem_limit_bytes=VMEM_LIMIT),
    )(*kept(pltpu.VMEM, mine, store))


def score(known, theirs, store, width, doc_count):
    vmem = pl.BlockSpec(memory_space=pltpu.VMEM)
    slabs = width // LANES * store.shape[0] // LANES
    return pl.pallas_call(
        functools.partial(score_kernel, width),
        out_shape=jax.ShapeDtypeStruct((doc_count, store.shape[0]), jnp.float32),
        in_specs=[vmem] * 3,
        out_specs=vmem,
        scratch_shapes=[pltpu.VMEM((slabs * known.shape[0], LANES), jnp.float32)],
        compiler_params=pltpu.CompilerParams(vmem_limit_bytes=VMEM_LIMIT),
    )(*kept(pltpu.VMEM, known, theirs, store))


def shards(activations, gradients, doc_ids, proj_in, proj_out, inverse, store_rows):
    ctx = lax.axis_size("ctx")
    rank = proj_in.shape[1]
    half = rank // lax.axis_size("col")
    doc_count = SLOTS * ctx // 2
    part, mask, numbers = project(activations, gradients, proj_in, proj_out, doc_ids)
    sums, tags = outer(part, swap_cores(part), mask, numbers)
    blocks, tags = sums.astype(jnp.float16), tags.astype(jnp.float16)
    depth = inverse.shape[0]
    turns = len(plans()[0])
    cuts = [0] + [depth * k // 8 // LANES * LANES for k in (2, 5)] + [depth]
    highs, lows = [], []

    def beside(payload, turn, ready):
        other, at = exchange(payload, turn), len(highs)
        pair = fetch(inverse, cuts[at], cuts[at + 1] - cuts[at], ready)
        other, high, low = lax.optimization_barrier((other, *pair))
        highs.append(high)
        lows.append(low)
        return other

    for turn in range(turns - 1):
        size = blocks.shape[0]
        payload = jnp.concatenate([blocks, tags])
        if turn < turns - 3:
            other = exchange(payload, turn)
        else:
            other = beside(payload, turn, tags.astype(jnp.float32))
        if turn < turns - 2:
            blocks = jnp.concatenate([blocks, other[:size]])
            tags = tags + jnp.roll(other[size:], SLOTS << turn, 1)
        else:
            tags = tags + jnp.roll(other[size:], 2, 0)
    first = lax.axis_index("col") == 0
    own, others = [], []
    for part in (blocks, other[:size]):
        halves = part.reshape(-1, 2, half * rank // LANES, LANES)
        own.append(jnp.where(first, halves[:, 0], halves[:, 1]).reshape(-1, LANES))
        others.append(jnp.where(first, halves[:, 1], halves[:, 0]).reshape(-1, LANES))
    own, others = jnp.concatenate(own), jnp.concatenate(others)
    own = jnp.concatenate([own, tags]).astype(jnp.float32)
    other = beside(jnp.concatenate([others, tags]), turns - 1, own)
    partial_q = precondition(own, other.astype(jnp.float32), highs, lows, doc_count)
    precond = (partial_q + swap_cores(partial_q)).astype(jnp.bfloat16)
    width = precond.shape[1]
    whole = precond.reshape(-1, min(width, LANES))
    count = store_rows.shape[0]
    direct = width % LANES == 0 and LANES % count == 0 and width * count % LANES**2 == 0
    if direct:
        store = load(store_rows, whole)
    for turn in range(turns - 1):
        other = exchange(whole, turn)
        if direct and turn == 0:
            other, store = lax.optimization_barrier((other, store))
        whole = jnp.concatenate([whole, other])
    others = exchange(whole, turns - 1)
    if direct:
        known = score_held(whole, store, width, doc_count)
        others, known = lax.optimization_barrier((others, known))
        return score(known, others, store, width, doc_count)
    whole = jnp.concatenate([whole, others]).reshape(ctx, doc_count, width)
    owners = jnp.stack([owner(place) for place in range(ctx)])
    found = owners[None, :] == jnp.arange(ctx, dtype=owners.dtype)[:, None]
    whole = jnp.take(whole, jnp.argmax(found, axis=1), axis=0)
    whole = whole.transpose(1, 0, 2).reshape(doc_count, -1)
    return lax.dot_general(
        whole, store_rows, (((1,), (1,)), ((), ())), preferred_element_type=jnp.float32
    )


def solution(mesh):
    in_specs = (
        P(("groups", "ctx"), "col"),
        P(("groups", "ctx"), "col"),
        P(("groups", "ctx")),
        P("col", None),
        P("col", None),
        P("col", "ctx"),
        P(("groups", "ctx", "col"), None),
    )
    out_specs = P(None, ("groups", "ctx", "col"))
    return jax.shard_map(shards, mesh=mesh, in_specs=in_specs, out_specs=out_specs, check_vma=False)
```
